32 devices in a mesh: outer: 4 (over y, core), inner: 8 (over z, x).
Axes of the slice: x: 2, y: 2, z: 4, core: 2. Of those that a mesh axis runs over, the one named last changes fastest.
Arguments:
- queries: bfloat16 [8192, 1024], P(('outer', 'inner')), may hold values from -100 to 100
- keys: bfloat16 [8192, 1024], P(('outer', 'inner')), may hold values from -6 to 6
- values: bfloat16 [8192, 1024], P(('outer', 'inner')), may hold values from -6 to 6
- modality: int32 [8192], P(('outer', 'inner')), may hold values 0 or 1
Outputs:
- attended: bfloat16 [8192, 1024], P(('outer', 'inner'))
The draws below stay inside these ranges and needn't reach their ends.
All inputs are finite; a program needn't handle non-finite values. No bound on the sum of `modality` on one device may be relied on, other than what follows from the above.
Results may differ from the reference program's by a relative error of at most 0.0034.
Values may be sent and summed in bfloat16 or wider, within the bound.
A program may use at most 128 MiB of HBM per device.

```python
import math
import jax
import jax.numpy as jnp
from jax import lax

HEADS = 8
HEAD_DIM = 128
BLOCK = 128
TOK_DEV = 256
DM = 1024
TOKENS = 8192
LEVELS = 5


def smooth_field(key):
    freq_key, phase_key = jax.random.split(key)
    device_total = TOKENS // TOK_DEV
    top_power = max(device_total.bit_length() - 1, 1)
    powers = jax.random.randint(freq_key, (DM,), 0, top_power)
    cycles = jnp.left_shift(jnp.ones((DM,), jnp.int32), powers)
    offsets = jax.random.uniform(phase_key, (DM,), jnp.float32, -math.pi, math.pi)
    places = jnp.arange(TOKENS, dtype=jnp.int32)
    turns = places[:, None] * cycles[None, :] % TOKENS
    return jnp.sin(turns.astype(jnp.float32) * (2.0 * math.pi / TOKENS) + offsets[None, :])


def base_keys(key):
    noise_key, smooth_key = jax.random.split(jax.random.fold_in(key, 11), 2)
    rough = jax.random.truncated_normal(noise_key, -4.0, 4.0, (TOKENS, DM), jnp.float32)
    return rough + smooth_field(smooth_key)


def draw_keys(key, part):
    return base_keys(key).astype(jnp.bfloat16)


def draw_queries(key, part):
    query_key = jax.random.fold_in(jax.random.fold_in(key, 23), 0)
    return jax.random.truncated_normal(query_key, -4.0, 4.0, (TOKENS, DM), jnp.float32).astype(jnp.bfloat16)


def draw_values(key, part):
    noise_key, smooth_key = jax.random.split(jax.random.fold_in(key, 37), 2)
    rough = jax.random.truncated_normal(noise_key, -4.0, 4.0, (TOKENS, DM), jnp.float32)
    return (rough + smooth_field(smooth_key)).astype(jnp.bfloat16)


def place_ends(entries, key, low, top_value):
    dims = entries.shape
    place = [jax.random.randint(jax.random.fold_in(key, axis), (), 0, dims[axis]) for axis in range(len(dims))]
    entries = entries.at[tuple(place)].set(low)
    longest = dims.index(max(dims))
    place[longest] = (place[longest] + 1) % dims[longest]
    return entries.at[tuple(place)].set(top_value)


def setup_inputs(seed: int = 0) -> dict:
    key_list = jax.random.split(jax.random.key(seed), 5)
    return {
        "queries": draw_queries(jax.random.fold_in(key_list[4], 71), 0),
        "keys": draw_keys(jax.random.fold_in(key_list[4], 71), 0),
        "values": draw_values(jax.random.fold_in(key_list[4], 71), 0),
        "modality": place_ends((jax.random.randint(key_list[3], (TOKENS,), 0, 3) < 1).astype(jnp.int32), jax.random.fold_in(key_list[3], 1), 0, 1),
    }


def coarsen(rows_in):
    paired = rows_in.astype(jnp.float32).reshape(rows_in.shape[0] // 2, 2, rows_in.shape[1])
    return (0.5 * (paired[:, 0] + paired[:, 1])).astype(jnp.bfloat16)


def reference(queries, keys, values, modality):
    key_levels = []
    value_levels = []
    key_now = keys
    value_now = values
    for level in range(LEVELS):
        key_now = coarsen(key_now)
        value_now = coarsen(value_now)
        key_levels.append(key_now)
        value_levels.append(value_now)
    key_pad = jnp.pad(keys, ((BLOCK, BLOCK), (0, 0)))
    value_pad = jnp.pad(values, ((BLOCK, BLOCK), (0, 0)))
    label_pad = jnp.pad(modality, (BLOCK, BLOCK), constant_values=-1)
    score_scale = HEAD_DIM ** -0.5
    columns = jnp.arange(3 * BLOCK, dtype=jnp.int32)
    middle = (columns >= BLOCK) & (columns < 2 * BLOCK)

    def one_block(block_index):
        start = (block_index * BLOCK).astype(jnp.int32)
        query_rows = lax.dynamic_slice_in_dim(queries, start, BLOCK, 0).astype(jnp.float32)
        query_rows = query_rows.reshape(BLOCK, HEADS, HEAD_DIM)
        key_parts = [lax.dynamic_slice_in_dim(key_pad, start, 3 * BLOCK, 0)]
        value_parts = [lax.dynamic_slice_in_dim(value_pad, start, 3 * BLOCK, 0)]
        key_labels = lax.dynamic_slice_in_dim(label_pad, start, 3 * BLOCK, 0)
        query_labels = lax.dynamic_slice_in_dim(modality, start, BLOCK, 0)
        near_mask = (key_labels[None, :] == query_labels[:, None]) | middle[None, :]
        allowed = jnp.concatenate([near_mask, jnp.ones((BLOCK, LEVELS * BLOCK), bool)], axis=1)
        for level in range(LEVELS):
            node_index = block_index // (2 ** (level + 1))
            sibling = (node_index + 1 - 2 * (node_index % 2)).astype(jnp.int32)
            key_parts.append(lax.dynamic_slice_in_dim(key_levels[level], sibling * BLOCK, BLOCK, 0))
            value_parts.append(lax.dynamic_slice_in_dim(value_levels[level], sibling * BLOCK, BLOCK, 0))
        all_keys = jnp.concatenate(key_parts, axis=0).astype(jnp.float32).reshape(-1, HEADS, HEAD_DIM)
        all_values = jnp.concatenate(value_parts, axis=0).astype(jnp.float32).reshape(-1, HEADS, HEAD_DIM)
        logits = jnp.einsum("qhd,khd->hqk", query_rows, all_keys) * score_scale
        logits = jnp.where(allowed[None], logits, -jnp.inf)
        row_top = jnp.max(logits, axis=2, keepdims=True)
        weights = jnp.exp(logits - row_top)
        denominator = jnp.sum(weights, axis=2)
        rounded = lax.optimization_barrier(weights.astype(jnp.bfloat16)).astype(jnp.float32)
        numerator = jnp.einsum("hqk,khd->qhd", rounded, all_values)
        result = numerator / denominator.T[:, :, None]
        return result.reshape(BLOCK, HEADS * HEAD_DIM).astype(jnp.bfloat16)

    block_ids = jnp.arange(TOKENS // BLOCK, dtype=jnp.int32)
    outputs = lax.map(one_block, block_ids, batch_size=16)
    return outputs.reshape(TOKENS, HEADS * HEAD_DIM)
```

```python
import functools
import math

import jax
import jax.numpy as jnp
from jax import lax
from jax.experimental import pallas as pl
from jax.experimental.pallas import tpu as pltpu
from jax.sharding import PartitionSpec as P

HEAD_DIM = 128
BLOCK = 128
AXES = ("outer", "inner")
MESH = pl.DeviceIdType.MESH
F32 = jnp.float32
BF16 = jnp.bfloat16


def pair_means(rows):
    half = rows.shape[0] // 2
    r = lax.broadcasted_iota(jnp.int32, (half, rows.shape[0]), 0)
    c = lax.broadcasted_iota(jnp.int32, (half, rows.shape[0]), 1)
    mix = jnp.where(c // 2 == r, 0.5, 0.0).astype(BF16)
    return jnp.dot(mix, rows, preferred_element_type=F32).astype(BF16)


def kernel(
    levels, inner, q_hbm, k_hbm, v_hbm, mod_hbm, out_ref,
    q_ref, k_ref, v_ref, mod_ref, node, far, mate, mate_mod, cross, cross_mod,
    bias_own, bias_near, m_ref, l_ref, acc_ref,
    load_sem, far_send, far_recv, mate_send, mate_recv, cross_send, cross_recv,
):
    rows, width = q_ref.shape
    heads = width // HEAD_DIM
    half = BLOCK // 2
    quarter = BLOCK // 4
    count = 2**levels
    me = lax.axis_index("outer") * inner + lax.axis_index("inner")
    scale = HEAD_DIM**-0.5 * math.log2(math.e)
    own = (k_ref, v_ref)

    def place(d):
        return (d // inner, d % inner)

    def bit(b):
        return me // 2**b % 2

    def flip(b):
        return me + 2**b * (1 - 2 * bit(b))

    odd = bit(0)
    hop_out = jnp.where(odd == 0, (me + 2) % count, (me + count - 2) % count)
    hop_in = jnp.where(odd == 0, (me + count - 2) % count, (me + 2) % count)
    gives = ((odd == 0) & (me + 2 < count)) | ((odd == 1) & (me > 2))
    takes = ((odd == 0) & (me > 0)) | ((odd == 1) & (me + 1 < count))

    barrier = pltpu.get_barrier_semaphore()
    for target in [flip(b) for b in range(levels)] + [hop_out, hop_in]:
        pl.semaphore_signal(barrier, inc=1, device_id=place(target), device_id_type=MESH)

    loads = [
        pltpu.make_async_copy(src, dst, load_sem.at[i])
        for i, (src, dst) in enumerate(
            ((k_hbm, k_ref), (v_hbm, v_ref), (mod_hbm, mod_ref), (q_hbm, q_ref))
        )
    ]
    for load in loads:
        load.start()

    def span(start, size):
        return pl.ds(pl.multiple_of(start, size), size)

    def half_rows(upper):
        return span(upper * half, half)

    def quarter_rows(upper, lower):
        return span(upper * half + lower * quarter, quarter)

    def own_half(b, part):
        node[b, part, half_rows(bit(b - 1)), :] = pair_means(node[b - 1, part])

    def other_half(b, part):
        node[b, part, half_rows(1 - bit(b - 1)), :] = pair_means(far[b - 1, part])

    for part in range(2):
        loads[part].wait()
        two = pair_means(pair_means(own[part][...]))
        node[1, part, half_rows(odd), :] = two
        node[2, part, quarter_rows(bit(1), odd), :] = pair_means(two)

    @pl.when(~takes)
    def _():
        cross[...] = jnp.zeros(cross.shape, BF16)
        cross_mod[...] = jnp.full(cross_mod.shape, -1, jnp.int32)

    pl.semaphore_wait(barrier, levels + 2)

    def remote(src, dst, send, recv, target):
        return pltpu.make_async_remote_copy(
            src_ref=src, dst_ref=dst, send_sem=send, recv_sem=recv,
            device_id=place(target), device_id_type=MESH,
        )

    def level_copy(b, part, slot, view, target, src=None):
        src = node if src is None else src
        return remote(src.at[b, part, view], far.at[b, part, view],
                      far_send.at[b, part, slot], far_recv.at[b, part, slot], target)

    def whole_copy(b, part):
        return level_copy(b, part, 0, pl.ds(0, BLOCK), flip(b))

    def half_copy(b, part):
        return level_copy(b, part, 0, half_rows(bit(b - 1)), flip(b))

    def share_copy(b, part):
        return level_copy(b, part, 1, half_rows(bit(b - 1)), flip(b - 1), far)

    def early_view(slot):
        return quarter_rows(bit(3), bit(2) if slot == 0 else 1 - bit(2))

    def quarter_copy(part, slot):
        return level_copy(4, part, slot, early_view(slot), flip(4))

    def quarter_share(part, slot):
        return level_copy(4, part, 2 + slot, early_view(slot), flip(3), far)

    def three_copy(part):
        view = node.at[2, part, quarter_rows(bit(1), odd)]
        return remote(view, view, mate_send.at[part, 2], mate_recv.at[part, 2], flip(0))

    def block_rows(i):
        return span(i * BLOCK, BLOCK)

    def mate_copy(part, slot):
        view = block_rows(odd if slot == 0 else 1 - odd)
        return remote(own[part].at[view], mate.at[part, view],
                      mate_send.at[part, slot], mate_recv.at[part, slot], flip(0))

    def mod_copy():
        return remote(mod_ref, mate_mod, mate_send.at[2, 0], mate_recv.at[2, 0], flip(0))

    def hop_copy(part):
        return remote(mate.at[part, block_rows(1 - odd)], cross.at[part],
                      cross_send.at[part], cross_recv.at[part], hop_out)

    def hop_mod():
        return remote(mate_mod.at[1 - odd], cross_mod, cross_send.at[2], cross_recv.at[2], hop_out)

    for part in range(2):
        three_copy(part).start()
    for part in range(2):
        half_copy(1, part).start()
    mate_copy(0, 0).start()
    loads[2].wait()
    mod_copy().start()
    loads[3].wait()

    def label_rows(i):
        return jnp.broadcast_to(mod_ref[i].astype(F32), (BLOCK, BLOCK))

    labels = [label_rows(0), label_rows(1)]
    columns = [jnp.transpose(x) for x in labels]
    zero = jnp.zeros((BLOCK, BLOCK), F32)
    for i in range(2):
        for j in range(2):
            value = zero if i == j else jnp.where(labels[j] == columns[i], 0.0, -jnp.inf)
            bias_own[i * BLOCK : (i + 1) * BLOCK, j * BLOCK : (j + 1) * BLOCK] = value

    def head_cols(h):
        return pl.ds(pl.multiple_of(h * HEAD_DIM, HEAD_DIM), HEAD_DIM)

    def score(q, k):
        return lax.dot_general(q, k, (((1,), (1,)), ((), ())), preferred_element_type=F32) * scale

    def first(h):
        cols = head_cols(h)
        s = score(q_ref[:, cols], k_ref[:, cols]) + bias_own[...]
        m = jnp.broadcast_to(jnp.max(s, axis=1, keepdims=True), (rows, BLOCK))
        p0 = jnp.exp2(s[:, :BLOCK] - m)
        p1 = jnp.exp2(s[:, BLOCK:] - m)
        m_ref[h] = m
        l_ref[h] = p0 + p1
        p = jnp.concatenate([p0.astype(BF16), p1.astype(BF16)], axis=1)
        acc_ref[h] = jnp.dot(p, v_ref[:, cols], preferred_element_type=F32)

    def merged(h, view, k, v, bias):
        cols = head_cols(h)
        s = score(q_ref[view, cols], k[:, cols])
        if bias is not None:
            s = s + bias[...]
        m_old = m_ref[h, view]
        m = jnp.maximum(m_old, jnp.max(s, axis=1, keepdims=True))
        p = jnp.exp2(s - m)
        a = jnp.exp2(m_old - m)
        l = l_ref[h, view] * a + p
        acc = acc_ref[h, view] * a + jnp.dot(p.astype(BF16), v[:, cols], preferred_element_type=F32)
        return m, l, acc

    def update(h, view, k, v, bias=None):
        m, l, acc = merged(h, view, k, v, bias)
        m_ref[h, view] = m
        l_ref[h, view] = l
        acc_ref[h, view] = acc

    def every_head(body, low=0, high=heads):
        def step(h, carry):
            body(h)
            return carry

        lax.fori_loop(low, high, step, 0, unroll=8)

    everything = pl.ds(0, rows)

    def near_update(side, label, k, v, slot):
        view = block_rows(side)
        other = jnp.broadcast_to(label.astype(F32), (BLOCK, BLOCK))
        mine = jnp.transpose(label_rows(side))
        bias_near[slot] = jnp.where(other == mine, 0.0, -jnp.inf)
        every_head(lambda h: update(h, view, k, v, bias_near.at[slot]))

    def far_head(b):
        return lambda h: update(h, everything, far.at[b, 0], far.at[b, 1])

    def last_head(b):
        def body(h):
            m, l, acc = merged(h, everything, far.at[b, 0], far.at[b, 1], None)
            total = jnp.sum(l, axis=1, keepdims=True)
            out_ref[:, head_cols(h)] = (acc / total).astype(BF16)

        return body

    def both(action):
        for part in range(2):
            action(part)

    def coarse_mate(part, slot):
        block = 1 - odd if slot == 0 else odd
        far[0, part, half_rows(block), :] = pair_means(mate[part, block_rows(block), :])

    every_head(first, 0, heads // 2)

    def pair_three(part):
        three_copy(part).wait_recv()
        half_copy(2, part).start()

    both(pair_three)
    every_head(first, heads // 2, heads)

    def share_two(part):
        half_copy(1, part).wait_recv()
        share_copy(1, part).start()

    both(share_two)
    mate_copy(1, 0).start()
    both(lambda part: mate_copy(part, 1).start())

    mate_copy(0, 0).wait_recv()
    mod_copy().wait_recv()

    @pl.when(gives)
    def _():
        hop_copy(0).start()
        hop_mod().start()

    coarse_mate(0, 0)

    def share_three(part):
        half_copy(2, part).wait_recv()
        share_copy(2, part).start()

    def two_ready(part):
        share_copy(1, part).wait_recv()
        other_half(2, part)
        own_half(3, part)
        if levels > 4:
            node[4, part, early_view(0), :] = pair_means(node[3, part, half_rows(bit(2)), :])
            quarter_copy(part, 0).start()

    share_three(0)
    two_ready(0)
    share_three(1)
    two_ready(1)
    every_head(far_head(1))

    mate_copy(1, 0).wait_recv()
    pl.when(gives)(lambda: hop_copy(1).start())
    coarse_mate(1, 0)

    def three_ready(part):
        share_copy(2, part).wait_recv()
        other_half(3, part)
        whole_copy(3, part).start()
        if levels > 4:
            node[4, part, early_view(1), :] = pair_means(node[3, part, half_rows(1 - bit(2)), :])
            quarter_copy(part, 1).start()

    both(three_ready)
    if levels > 4:
        both(lambda part: quarter_copy(part, 0).wait_recv())
        both(lambda part: quarter_share(part, 0).start())
    every_head(far_head(2))

    def four_ready(part):
        whole_copy(3, part).wait_recv()
        if levels > 5:
            other_half(4, part)
            own_half(5, part)

    both(four_ready)
    every_head(far_head(3))

    @pl.when(takes)
    def _():
        hop_mod().wait_recv()
        hop_copy(0).wait_recv()
        hop_copy(1).wait_recv()

    near_update(odd, cross_mod[...], cross.at[0], cross.at[1], 0)
    if levels > 4:
        both(lambda part: quarter_copy(part, 1).wait_recv())
        both(lambda part: quarter_share(part, 1).start())
    mate_copy(0, 1).wait_recv()
    coarse_mate(0, 1)
    if levels > 4:
        for slot in range(2):
            both(lambda part: quarter_share(part, slot).wait_recv())
        every_head(far_head(4))
    for b in range(5, levels):
        for part in range(2):
            other_half(b, part)
            whole_copy(b, part).start()
            whole_copy(b, part).wait_recv()
            if b + 1 < levels:
                own_half(b + 1, part)
        every_head(far_head(b))
    mate_copy(1, 1).wait_recv()
    coarse_mate(1, 1)
    near = block_rows(odd)
    near_update(1 - odd, mate_mod[odd], mate.at[0, near], mate.at[1, near], 1)
    every_head(last_head(0))

    @pl.when(gives)
    def _():
        both(lambda part: hop_copy(part).wait_send())
        hop_mod().wait_send()

    mod_copy().wait_send()
    for part in range(2):
        three_copy(part).wait_send()
        for slot in range(2):
            mate_copy(part, slot).wait_send()
        for b in (1, 2):
            half_copy(b, part).wait_send()
            share_copy(b, part).wait_send()
        whole_copy(3, part).wait_send()
        for slot in range(2):
            if levels > 4:
                quarter_copy(part, slot).wait_send()
                quarter_share(part, slot).wait_send()
        for b in range(5, levels):
            whole_copy(b, part).wait_send()


def shards(levels, inner, queries, keys, values, modality):
    rows, width = queries.shape
    heads = width // HEAD_DIM
    labels = modality.reshape(rows // BLOCK, 1, BLOCK)
    hbm = pl.BlockSpec(memory_space=pl.ANY)
    state = pltpu.VMEM((heads, rows, HEAD_DIM), F32)
    shard = pltpu.VMEM((rows, width), BF16)
    level = pltpu.VMEM((levels, 2, BLOCK, width), BF16)
    label = pltpu.VMEM((rows // BLOCK, 1, BLOCK), jnp.int32)
    return pl.pallas_call(
        functools.partial(kernel, levels, inner),
        out_shape=jax.ShapeDtypeStruct((rows, width), BF16),
        in_specs=[hbm] * 4,
        out_specs=pl.BlockSpec(memory_space=pltpu.VMEM),
        scratch_shapes=[
            shard,
            shard,
            shard,
            label,
            level,
            level,
            pltpu.VMEM((2, rows, width), BF16),
            label,
            pltpu.VMEM((2, BLOCK, width), BF16),
            pltpu.VMEM((1, BLOCK), jnp.int32),
            pltpu.VMEM((rows, 2 * BLOCK), F32),
            pltpu.VMEM((2, BLOCK, BLOCK), F32),
            state,
            state,
            state,
            pltpu.SemaphoreType.DMA((4,)),
            pltpu.SemaphoreType.DMA((levels, 2, 4)),
            pltpu.SemaphoreType.DMA((levels, 2, 4)),
            pltpu.SemaphoreType.DMA((3, 3)),
            pltpu.SemaphoreType.DMA((3, 3)),
            pltpu.SemaphoreType.DMA((3,)),
            pltpu.SemaphoreType.DMA((3,)),
        ],
        compiler_params=pltpu.CompilerParams(
            collective_id=0, has_side_effects=True, vmem_limit_bytes=56 * 2**20
        ),
    )(queries, keys, values, labels)


def solution(mesh):
    outer, inner = mesh.shape["outer"], mesh.shape["inner"]
    levels = (outer * inner).bit_length() - 1
    rows = P(AXES, None)
    return jax.shard_map(
        functools.partial(shards, levels, inner),
        mesh=mesh,
        in_specs=(rows, rows, rows, P(AXES)),
        out_specs=rows,
        check_vma=False,
    )
```

```python
import functools
import math

import jax
import jax.numpy as jnp
from jax import lax
from jax.experimental import pallas as pl
from jax.experimental.pallas import tpu as pltpu
from jax.sharding import PartitionSpec as P

HEAD_DIM = 128
BLOCK = 128
AXES = ("outer", "inner")
MESH = pl.DeviceIdType.MESH
GROUPS = 4
F32 = jnp.float32
BF16 = jnp.bfloat16


def pair_means(rows):
    half = rows.shape[0] // 2
    r = lax.broadcasted_iota(jnp.int32, (half, rows.shape[0]), 0)
    c = lax.broadcasted_iota(jnp.int32, (half, rows.shape[0]), 1)
    mix = jnp.where(c // 2 == r, 0.5, 0.0).astype(BF16)
    return jnp.dot(mix, rows, preferred_element_type=F32).astype(BF16)


def kernel(
    levels, inner, q_hbm, k_hbm, v_hbm, mod_hbm, out_ref,
    q_ref, k_ref, v_ref, mod_ref, node, far, mate, mate_mod, cross, cross_mod,
    bias_own, bias_near, m_ref, l_ref, acc_ref,
    ready, load_sem, far_send, far_recv, mate_send, mate_recv, cross_send, cross_recv,
):
    rows, width = q_ref.shape
    heads = width // HEAD_DIM
    groups = min(GROUPS, heads)
    half = BLOCK // 2
    quarter = BLOCK // 4
    count = 2**levels
    me = lax.axis_index("outer") * inner + lax.axis_index("inner")
    scale = HEAD_DIM**-0.5 * math.log2(math.e)
    own = (k_ref, v_ref)

    def place(d):
        return (d // inner, d % inner)

    def bit(b):
        return me // 2**b % 2

    def flip(b):
        return me + 2**b * (1 - 2 * bit(b))

    odd = bit(0)
    hop_out = jnp.where(odd == 0, (me + 2) % count, (me + count - 2) % count)
    gives = ((odd == 0) & (me + 2 < count)) | ((odd == 1) & (me > 2))
    takes = ((odd == 0) & (me > 0)) | ((odd == 1) & (me + 1 < count))

    barrier = pltpu.get_barrier_semaphore()
    for b in range(levels):
        pl.semaphore_signal(barrier, inc=1, device_id=place(flip(b)), device_id_type=MESH)

    loads = [
        pltpu.make_async_copy(src, dst, load_sem.at[i])
        for i, (src, dst) in enumerate(
            ((k_hbm, k_ref), (v_hbm, v_ref), (mod_hbm, mod_ref), (q_hbm, q_ref))
        )
    ]
    for load in loads:
        load.start()

    def span(start, size):
        return pl.ds(pl.multiple_of(start, size), size)

    def half_rows(upper):
        return span(upper * half, half)

    def quarter_rows(upper, lower):
        return span(upper * half + lower * quarter, quarter)

    def own_half(b, part):
        node[b, part, half_rows(bit(b - 1)), :] = pair_means(node[b - 1, part])

    def other_half(b, part):
        node[b, part, half_rows(1 - bit(b - 1)), :] = pair_means(far[b - 1, part])

    for part in range(2):
        loads[part].wait()
        two = pair_means(pair_means(own[part][...]))
        node[1, part, half_rows(odd), :] = two
        node[2, part, quarter_rows(bit(1), odd), :] = pair_means(two)

    @pl.when(~takes)
    def _():
        cross[...] = jnp.zeros(cross.shape, BF16)
        cross_mod[...] = jnp.full(cross_mod.shape, -1, jnp.int32)

    pl.semaphore_wait(barrier, levels)

    def greet(b):
        if b > 0:
            pl.semaphore_wait(ready.at[b - 1], 1)
        if b < levels:
            pl.semaphore_signal(ready.at[b], inc=1, device_id=place(flip(b)), device_id_type=MESH)

    def remote(src, dst, send, recv, target):
        return pltpu.make_async_remote_copy(
            src_ref=src, dst_ref=dst, send_sem=send, recv_sem=recv,
            device_id=place(target), device_id_type=MESH,
        )

    def level_copy(b, part, slot, view, target, src=None):
        src = node if src is None else src
        return remote(src.at[b, part, view], far.at[b, part, view],
                      far_send.at[b, part, slot], far_recv.at[b, part, slot], target)

    def whole_copy(b, part):
        return level_copy(b, part, 0, pl.ds(0, BLOCK), flip(b))

    def half_copy(b, part):
        return level_copy(b, part, 0, half_rows(bit(b - 1)), flip(b))

    def share_copy(b, part):
        return level_copy(b, part, 1, half_rows(bit(b - 1)), flip(b - 1), far)

    def three_view(slot):
        return quarter_rows(bit(1), odd if slot == 0 else 1 - odd)

    def five_view(slot):
        return quarter_rows(bit(3), bit(2) if slot == 0 else 1 - bit(2))

    def quarter_copy(b, part, slot):
        view = three_view(slot) if b == 2 else five_view(slot)
        return level_copy(b, part, slot, view, flip(b))

    def quarter_share(b, part, slot):
        view = three_view(slot) if b == 2 else five_view(slot)
        return level_copy(b, part, 2 + slot, view, flip(b - 1), far)

    def three_copy(part):
        view = node.at[2, part, quarter_rows(bit(1), odd)]
        return remote(view, view, mate_send.at[part, groups + 1], mate_recv.at[part, groups + 1], flip(0))

    def group_cols(g):
        return pl.ds(g * (width // groups), width // groups)

    def block_rows(i):
        return span(i * BLOCK, BLOCK)

    def mate_copy(part, slot):
        if slot == 0:
            view = (block_rows(odd), pl.ds(0, width))
        else:
            view = (block_rows(1 - odd), group_cols(slot - 1))
        return remote(own[part].at[view], mate.at[(part, *view)],
                      mate_send.at[part, slot], mate_recv.at[part, slot], flip(0))

    def mod_copy():
        return remote(mod_ref, mate_mod, mate_send.at[2, 0], mate_recv.at[2, 0], flip(0))

    def hop_copy(part, g):
        cols = pl.ds(0, width) if part == 0 else group_cols(g)
        return remote(mate.at[part, block_rows(1 - odd), cols], cross.at[part, :, cols],
                      cross_send.at[part, g], cross_recv.at[part, g], hop_out)

    def hop_copies(part):
        return [hop_copy(part, g) for g in range(groups if part else 1)]

    def hop_mod():
        return remote(mate_mod.at[1 - odd], cross_mod, cross_send.at[2, 0], cross_recv.at[2, 0], hop_out)

    loads[2].wait()
    for part in range(2):
        three_copy(part).start()
    for part in range(2):
        quarter_copy(2, part, 0).start()
    for part in range(2):
        half_copy(1, part).start()
    mod_copy().start()
    for part in range(2):
        mate_copy(part, 0).start()
    greet(0)
    loads[3].wait()

    def label_rows(i):
        return jnp.broadcast_to(mod_ref[i].astype(F32), (BLOCK, BLOCK))

    labels = [label_rows(0), label_rows(1)]
    columns = [jnp.transpose(x) for x in labels]
    zero = jnp.zeros((BLOCK, BLOCK), F32)
    for i in range(2):
        for j in range(2):
            value = zero if i == j else jnp.where(labels[j] == columns[i], 0.0, -jnp.inf)
            bias_own[i * BLOCK : (i + 1) * BLOCK, j * BLOCK : (j + 1) * BLOCK] = value

    def head_cols(h):
        return pl.ds(pl.multiple_of(h * HEAD_DIM, HEAD_DIM), HEAD_DIM)

    def score(q, k):
        return lax.dot_general(q, k, (((1,), (1,)), ((), ())), preferred_element_type=F32) * scale

    def first(h):
        cols = head_cols(h)
        s = score(q_ref[:, cols], k_ref[:, cols]) + bias_own[...]
        m = jnp.broadcast_to(jnp.max(s, axis=1, keepdims=True), (rows, BLOCK))
        p0 = jnp.exp2(s[:, :BLOCK] - m)
        p1 = jnp.exp2(s[:, BLOCK:] - m)
        m_ref[h] = m
        l_ref[h] = p0 + p1
        p = jnp.concatenate([p0.astype(BF16), p1.astype(BF16)], axis=1)
        acc_ref[h] = jnp.dot(p, v_ref[:, cols], preferred_element_type=F32)

    def merged(h, view, sources):
        cols = head_cols(h)
        q = q_ref[view, cols]
        scores = []
        for k, v, bias in sources:
            s = score(q, k[:, cols])
            scores.append(s if bias is None else s + bias[...])
        best = functools.reduce(jnp.maximum, scores)
        m_old = m_ref[h, view]
        m = jnp.maximum(m_old, jnp.max(best, axis=1, keepdims=True))
        a = jnp.exp2(m_old - m)
        weights = [jnp.exp2(s - m) for s in scores]
        l = l_ref[h, view] * a + functools.reduce(jnp.add, weights)
        p = jnp.concatenate([w.astype(BF16) for w in weights], axis=1)
        rows_in = jnp.concatenate([v[:, cols] for k, v, bias in sources], axis=0)
        acc = acc_ref[h, view] * a + jnp.dot(p, rows_in, preferred_element_type=F32)
        return m, l, acc

    def update(h, view, sources):
        m, l, acc = merged(h, view, sources)
        m_ref[h, view] = m
        l_ref[h, view] = l
        acc_ref[h, view] = acc

    def finish(h, view, sources):
        m, l, acc = merged(h, view, sources)
        total = jnp.sum(l, axis=1, keepdims=True)
        out_ref[view, head_cols(h)] = (acc / total).astype(BF16)

    def every_head(body, low=0, high=heads):
        def step(h, carry):
            body(h)
            return carry

        lax.fori_loop(low, high, step, 0, unroll=8)

    everything = pl.ds(0, rows)

    def near_bias(side, label, slot):
        other = jnp.broadcast_to(label.astype(F32), (BLOCK, BLOCK))
        mine = jnp.transpose(label_rows(side))
        bias_near[slot] = jnp.where(other == mine, 0.0, -jnp.inf)
        return bias_near.at[slot]

    def level_rows(b):
        return (far.at[b, 0], far.at[b, 1], None)

    def both(action):
        for part in range(2):
            action(part)

    def coarse_mate(part, slot):
        block = 1 - odd if slot == 0 else odd
        cols = pl.ds(0, width) if slot == 0 else group_cols(slot - 1)
        far[0, part, half_rows(block), cols] = pair_means(mate[part, block_rows(block), cols])

    def pair_three(part):
        three_copy(part).wait_recv()
        quarter_copy(2, part, 1).start()

    def share_two(part):
        half_copy(1, part).wait_recv()
        share_copy(1, part).start()

    def share_three(slot):
        for part in range(2):
            quarter_copy(2, part, slot).wait_recv()
            quarter_share(2, part, slot).start()

    def two_ready(part):
        share_copy(1, part).wait_recv()
        other_half(2, part)
        own_half(3, part)
        other_half(3, part)
        whole_copy(3, part).start()
        if levels > 4:
            for slot in range(2):
                half_of = half_rows(bit(2) if slot == 0 else 1 - bit(2))
                node[4, part, five_view(slot), :] = pair_means(node[3, part, half_of, :])
                quarter_copy(4, part, slot).start()

    def four_ready(part):
        whole_copy(3, part).wait_recv()
        if levels > 5:
            other_half(4, part)
            own_half(5, part)

    def share_five(slot):
        if levels > 4:
            for part in range(2):
                quarter_copy(4, part, slot).wait_recv()
                quarter_share(4, part, slot).start()

    def relay(part):
        mate_copy(part, 0).wait_recv()

        @pl.when(gives)
        def _():
            if part == 0:
                hop_mod().start()
            for copy in hop_copies(part):
                copy.start()

    parts = 4

    def first_part(i):
        every_head(first, heads * i // parts, heads * (i + 1) // parts)

    first_part(0)
    greet(1)
    first_part(1)
    both(pair_three)
    greet(2)
    first_part(2)
    share_three(0)
    greet(3)
    first_part(3)
    both(share_two)
    for g in range(groups):
        both(lambda part: mate_copy(part, g + 1).start())
    for b in range(4, levels + 1):
        greet(b)
    share_three(1)
    mod_copy().wait_recv()
    relay(0)
    coarse_mate(0, 0)
    relay(1)
    coarse_mate(1, 0)
    beside = near_bias(1 - odd, mate_mod[odd], 1)
    for slot in range(2):
        both(lambda part: quarter_share(2, part, slot).wait_recv())
    every_head(lambda h: update(h, everything, [level_rows(2)]))
    both(two_ready)
    both(four_ready)
    every_head(lambda h: update(h, everything, [level_rows(1), level_rows(3)]))
    share_five(0)
    share_five(1)

    @pl.when(takes)
    def _():
        hop_mod().wait_recv()
        hop_copy(0, 0).wait_recv()

    across = near_bias(odd, cross_mod[...], 0)
    last = []
    if levels > 4:
        for slot in range(2):
            both(lambda part: quarter_share(4, part, slot).wait_recv())
        last.append(level_rows(4))
    for b in range(5, levels):
        for part in range(2):
            other_half(b, part)
            whole_copy(b, part).start()
            whole_copy(b, part).wait_recv()
            if b + 1 < levels:
                own_half(b + 1, part)
        last.append(level_rows(b))
    if last:
        every_head(lambda h: update(h, everything, last))
    side = block_rows(odd)
    other_side = block_rows(1 - odd)
    cross_rows = (cross.at[0], cross.at[1], across)
    near_rows = (mate.at[0, side], mate.at[1, side], beside)
    for g in range(groups):
        for part in range(2):
            mate_copy(part, g + 1).wait_recv()
            coarse_mate(part, g + 1)
        pl.when(takes)(lambda: hop_copy(1, g).wait_recv())
        for h in range(heads * g // groups, heads * (g + 1) // groups):
            finish(h, other_side, [near_rows, level_rows(0)])
            finish(h, side, [cross_rows, level_rows(0)])

    @pl.when(gives)
    def _():
        for copy in hop_copies(0) + hop_copies(1):
            copy.wait_send()
        hop_mod().wait_send()

    mod_copy().wait_send()
    for part in range(2):
        three_copy(part).wait_send()
        for slot in range(groups + 1):
            mate_copy(part, slot).wait_send()
        half_copy(1, part).wait_send()
        share_copy(1, part).wait_send()
        whole_copy(3, part).wait_send()
        for b in (2, 4):
            for slot in range(2):
                if b < levels:
                    quarter_copy(b, part, slot).wait_send()
                    quarter_share(b, part, slot).wait_send()
        for b in range(5, levels):
            whole_copy(b, part).wait_send()


def shards(levels, inner, queries, keys, values, modality):
    rows, width = queries.shape
    heads = width // HEAD_DIM
    labels = modality.reshape(rows // BLOCK, 1, BLOCK)
    hbm = pl.BlockSpec(memory_space=pl.ANY)
    state = pltpu.VMEM((heads, rows, HEAD_DIM), F32)
    shard = pltpu.VMEM((rows, width), BF16)
    level = pltpu.VMEM((levels, 2, BLOCK, width), BF16)
    label = pltpu.VMEM((rows // BLOCK, 1, BLOCK), jnp.int32)
    return pl.pallas_call(
        functools.partial(kernel, levels, inner),
        out_shape=pltpu.VMEM((rows, width), BF16),
        in_specs=[hbm] * 4,
        out_specs=pl.BlockSpec(memory_space=pltpu.VMEM),
        scratch_shapes=[
            shard,
            shard,
            shard,
            label,
            level,
            level,
            pltpu.VMEM((2, rows, width), BF16),
            label,
            pltpu.VMEM((2, BLOCK, width), BF16),
            pltpu.VMEM((1, BLOCK), jnp.int32),
            pltpu.VMEM((rows, 2 * BLOCK), F32),
            pltpu.VMEM((2, BLOCK, BLOCK), F32),
            state,
            state,
            state,
            pltpu.SemaphoreType.REGULAR((levels,)),
            pltpu.SemaphoreType.DMA((4,)),
            pltpu.SemaphoreType.DMA((levels, 2, 4)),
            pltpu.SemaphoreType.DMA((levels, 2, 4)),
            pltpu.SemaphoreType.DMA((3, GROUPS + 2)),
            pltpu.SemaphoreType.DMA((3, GROUPS + 2)),
            pltpu.SemaphoreType.DMA((3, GROUPS)),
            pltpu.SemaphoreType.DMA((3, GROUPS)),
        ],
        compiler_params=pltpu.CompilerParams(
            collective_id=0, has_side_effects=True, vmem_limit_bytes=56 * 2**20
        ),
    )(queries, keys, values, labels)


def solution(mesh):
    outer, inner = mesh.shape["outer"], mesh.shape["inner"]
    levels = (outer * inner).bit_length() - 1
    rows = P(AXES, None)
    return jax.shard_map(
        functools.partial(shards, levels, inner),
        mesh=mesh,
        in_specs=(rows, rows, rows, P(AXES)),
        out_specs=rows,
        check_vma=False,
    )
```

```python
import functools
import math

import jax
import jax.numpy as jnp
from jax import lax
from jax.experimental import pallas as pl
from jax.experimental.pallas import tpu as pltpu
from jax.sharding import PartitionSpec as P

HEAD_DIM = 128
BLOCK = 128
AXES = ("outer", "inner")
MESH = pl.DeviceIdType.MESH
F32 = jnp.float32
BF16 = jnp.bfloat16


def pair_means(rows):
    half = rows.shape[0] // 2
    r = lax.broadcasted_iota(jnp.int32, (half, rows.shape[0]), 0)
    c = lax.broadcasted_iota(jnp.int32, (half, rows.shape[0]), 1)
    mix = jnp.where(c // 2 == r, 0.5, 0.0).astype(BF16)
    return jnp.dot(mix, rows, preferred_element_type=F32).astype(BF16)


def kernel(
    levels, inner, q_hbm, k_hbm, v_hbm, mod_hbm, out_ref,
    q_ref, k_ref, v_ref, mod_ref, node, far, mate, mate_mod, cross, cross_mod,
    bias_own, bias_near, m_ref, l_ref, acc_ref, p_near, p_coarse,
    ready, load_sem, far_send, far_recv, mate_send, mate_recv, cross_send, cross_recv,
):
    rows, width = q_ref.shape
    heads = width // HEAD_DIM
    half = BLOCK // 2
    quarter = BLOCK // 4
    count = 2**levels
    me = lax.axis_index("outer") * inner + lax.axis_index("inner")
    scale = HEAD_DIM**-0.5 * math.log2(math.e)
    own = (k_ref, v_ref)

    def place(d):
        return (d // inner, d % inner)

    def bit(b):
        return me // 2**b % 2

    def flip(b):
        return me + 2**b * (1 - 2 * bit(b))

    odd = bit(0)
    hop_out = jnp.where(odd == 0, (me + 2) % count, (me + count - 2) % count)
    gives = ((odd == 0) & (me + 2 < count)) | ((odd == 1) & (me > 2))
    takes = ((odd == 0) & (me > 0)) | ((odd == 1) & (me + 1 < count))

    barrier = pltpu.get_barrier_semaphore()
    for b in range(levels):
        pl.semaphore_signal(barrier, inc=1, device_id=place(flip(b)), device_id_type=MESH)

    def span(start, size):
        return pl.ds(pl.multiple_of(start, size), size)

    def block_rows(i):
        return span(i * BLOCK, BLOCK)

    def load(i, role):
        block = odd if role == 0 else 1 - odd
        src, dst = ((k_hbm, k_ref), (v_hbm, v_ref), (mod_hbm, mod_ref), (q_hbm, q_ref))[i]
        if i == 2:
            src, dst = src.at[block], dst.at[role]
        else:
            src, dst = src.at[block_rows(block)], dst.at[pl.ds(role * BLOCK, BLOCK)]
        return pltpu.make_async_copy(src, dst, load_sem.at[i, role])

    def loaded(i):
        load(i, 0).wait()
        load(i, 1).wait()

    for i in range(4):
        load(i, 0).start()
        load(i, 1).start()

    def half_rows(upper):
        return span(upper * half, half)

    def quarter_rows(upper, lower):
        return span(upper * half + lower * quarter, quarter)

    def own_half(b, part):
        node[b, part, half_rows(bit(b - 1)), :] = pair_means(node[b - 1, part])

    def other_half(b, part):
        node[b, part, half_rows(1 - bit(b - 1)), :] = pair_means(far[b - 1, part])

    for part in range(2):
        loaded(part)
        two = pair_means(pair_means(own[part][...]))
        node[1, part, half_rows(odd), :] = two
        node[2, part, quarter_rows(bit(1), odd), :] = pair_means(two)

    @pl.when(~takes)
    def _():
        cross[...] = jnp.zeros(cross.shape, BF16)
        cross_mod[...] = jnp.full(cross_mod.shape, -1, jnp.int32)

    pl.semaphore_wait(barrier, levels)

    def greet(b):
        if b > 0:
            pl.semaphore_wait(ready.at[b - 1], 1)
        if b < levels:
            pl.semaphore_signal(ready.at[b], inc=1, device_id=place(flip(b)), device_id_type=MESH)

    def remote(src, dst, send, recv, target):
        return pltpu.make_async_remote_copy(
            src_ref=src, dst_ref=dst, send_sem=send, recv_sem=recv,
            device_id=place(target), device_id_type=MESH,
        )

    def level_copy(b, part, slot, view, target, src=None):
        src = node if src is None else src
        return remote(src.at[b, part, view], far.at[b, part, view],
                      far_send.at[b, part, slot], far_recv.at[b, part, slot], target)

    def whole_copy(b, part):
        return level_copy(b, part, 0, pl.ds(0, BLOCK), flip(b))

    def half_copy(b, part):
        return level_copy(b, part, 0, half_rows(bit(b - 1)), flip(b))

    def share_copy(b, part):
        return level_copy(b, part, 1, half_rows(bit(b - 1)), flip(b - 1), far)

    def three_view(slot):
        return quarter_rows(bit(1), odd if slot == 0 else 1 - odd)

    def five_view(slot):
        return quarter_rows(bit(3), bit(2) if slot == 0 else 1 - bit(2))

    def quarter_copy(b, part, slot):
        view = three_view(slot) if b == 2 else five_view(slot)
        return level_copy(b, part, slot, view, flip(b))

    def quarter_share(b, part, slot):
        view = three_view(slot) if b == 2 else five_view(slot)
        return level_copy(b, part, 2 + slot, view, flip(b - 1), far)

    def three_copy(part):
        view = node.at[2, part, quarter_rows(bit(1), odd)]
        return remote(view, view, mate_send.at[part, 2], mate_recv.at[part, 2], flip(0))

    def mate_copy(part, role):
        view = pl.ds(role * BLOCK, BLOCK)
        return remote(own[part].at[view], mate.at[part, view],
                      mate_send.at[part, role], mate_recv.at[part, role], flip(0))

    def mod_copy():
        return remote(mod_ref, mate_mod, mate_send.at[2, 0], mate_recv.at[2, 0], flip(0))

    def hop_copy(part):
        return remote(mate.at[part, pl.ds(0, BLOCK)], cross.at[part],
                      cross_send.at[part], cross_recv.at[part], hop_out)

    def hop_mod():
        return remote(mate_mod.at[0], cross_mod, cross_send.at[2], cross_recv.at[2], hop_out)

    loaded(2)
    for part in range(2):
        three_copy(part).start()
    for part in range(2):
        quarter_copy(2, part, 0).start()
    for part in range(2):
        half_copy(1, part).start()
    mod_copy().start()
    for part in range(2):
        mate_copy(part, 0).start()
    greet(0)
    loaded(3)

    def label_rows(i):
        return jnp.broadcast_to(mod_ref[i].astype(F32), (BLOCK, BLOCK))

    labels = [label_rows(0), label_rows(1)]
    columns = [jnp.transpose(x) for x in labels]
    zero = jnp.zeros((BLOCK, BLOCK), F32)
    for i in range(2):
        for j in range(2):
            value = zero if i == j else jnp.where(labels[j] == columns[i], 0.0, -jnp.inf)
            bias_own[i * BLOCK : (i + 1) * BLOCK, j * BLOCK : (j + 1) * BLOCK] = value

    def head_cols(h):
        return pl.ds(pl.multiple_of(h * HEAD_DIM, HEAD_DIM), HEAD_DIM)

    def score(q, k):
        return lax.dot_general(q, k, (((1,), (1,)), ((), ())), preferred_element_type=F32) * scale

    def first(h):
        cols = head_cols(h)
        s = score(q_ref[:, cols], k_ref[:, cols]) + bias_own[...]
        m = jnp.broadcast_to(jnp.max(s, axis=1, keepdims=True), (rows, BLOCK))
        p0 = jnp.exp2(s[:, :BLOCK] - m)
        p1 = jnp.exp2(s[:, BLOCK:] - m)
        m_ref[h] = m
        l_ref[h] = p0 + p1
        p = jnp.concatenate([p0.astype(BF16), p1.astype(BF16)], axis=1)
        acc_ref[h] = jnp.dot(p, v_ref[:, cols], preferred_element_type=F32)

    def merged(h, view, sources):
        cols = head_cols(h)
        q = q_ref[view, cols]
        scores = []
        for k, v in sources:
            scores.append(score(q, k[:, cols]))
        best = functools.reduce(jnp.maximum, scores)
        m_old = m_ref[h, view]
        m = jnp.maximum(m_old, jnp.max(best, axis=1, keepdims=True))
        a = jnp.exp2(m_old - m)
        weights = [jnp.exp2(s - m) for s in scores]
        l = l_ref[h, view] * a + functools.reduce(jnp.add, weights)
        p = jnp.concatenate([w.astype(BF16) for w in weights], axis=1)
        rows_in = jnp.concatenate([v[:, cols] for k, v in sources], axis=0)
        acc = acc_ref[h, view] * a + jnp.dot(p, rows_in, preferred_element_type=F32)
        return m, l, acc

    def update(h, view, sources):
        m, l, acc = merged(h, view, sources)
        m_ref[h, view] = m
        l_ref[h, view] = l
        acc_ref[h, view] = acc

    def weigh(h):
        cols = head_cols(h)
        q = q_ref[:, cols]
        s = score(q, jnp.concatenate([cross[0, :, cols], mate[0, BLOCK:rows, cols]], axis=0))
        near = jnp.concatenate([s[:BLOCK, :BLOCK], s[BLOCK:, BLOCK:]], axis=0) + bias_near[...]
        coarse = score(q, far[0, 0, :, cols])
        m_old = m_ref[h]
        m = jnp.maximum(m_old, jnp.max(jnp.maximum(near, coarse), axis=1, keepdims=True))
        a = jnp.exp2(m_old - m)
        near = jnp.exp2(near - m)
        coarse = jnp.exp2(coarse - m)
        total = jnp.sum(l_ref[h] * a + near + coarse, axis=1, keepdims=True)
        l_ref[h] = jnp.broadcast_to(1.0 / total, (rows, HEAD_DIM))
        acc_ref[h] = acc_ref[h] * a
        near = near.astype(BF16)
        none = jnp.zeros((BLOCK, BLOCK), BF16)
        p_near[h, 0:BLOCK, :] = jnp.concatenate([near[:BLOCK], none], axis=1)
        p_near[h, BLOCK:rows, :] = jnp.concatenate([none, near[BLOCK:]], axis=1)
        p_coarse[h] = coarse.astype(BF16)

    def finish(h):
        cols = head_cols(h)
        beside = jnp.concatenate([cross[1, :, cols], mate[1, BLOCK:rows, cols]], axis=0)
        acc = acc_ref[h] + jnp.dot(p_near[h], beside, preferred_element_type=F32)
        acc = acc + jnp.dot(p_coarse[h], far[0, 1, :, cols], preferred_element_type=F32)
        acc = acc * l_ref[h]
        one, two = acc[:BLOCK], acc[BLOCK:]
        out_ref[0:BLOCK, cols] = jnp.where(odd == 0, one, two).astype(BF16)
        out_ref[BLOCK:rows, cols] = jnp.where(odd == 0, two, one).astype(BF16)

    def every_head(body, low=0, high=heads):
        def step(h, carry):
            body(h)
            return carry

        lax.fori_loop(low, high, step, 0, unroll=8)

    everything = pl.ds(0, rows)

    def near_bias(role, label):
        other = jnp.broadcast_to(label.astype(F32), (BLOCK, BLOCK))
        mine = jnp.transpose(label_rows(role))
        bias_near[role * BLOCK : (role + 1) * BLOCK, :] = jnp.where(other == mine, 0.0, -jnp.inf)

    def level_rows(b):
        return (far.at[b, 0], far.at[b, 1])

    def both(action):
        for part in range(2):
            action(part)

    def coarse_mate(part, role):
        far[0, part, role * half : (role + 1) * half, :] = pair_means(
            mate[part, role * BLOCK : (role + 1) * BLOCK, :]
        )

    def pair_three(part):
        three_copy(part).wait_recv()
        quarter_copy(2, part, 1).start()

    def share_two(part):
        half_copy(1, part).wait_recv()
        share_copy(1, part).start()

    def share_three(slot):
        for part in range(2):
            quarter_copy(2, part, slot).wait_recv()
            quarter_share(2, part, slot).start()

    def two_ready(part):
        share_copy(1, part).wait_recv()
        other_half(2, part)
        own_half(3, part)
        other_half(3, part)
        whole_copy(3, part).start()
        if levels > 4:
            for slot in range(2):
                half_of = half_rows(bit(2) if slot == 0 else 1 - bit(2))
                node[4, part, five_view(slot), :] = pair_means(node[3, part, half_of, :])
                quarter_copy(4, part, slot).start()

    def four_ready(part):
        whole_copy(3, part).wait_recv()
        if levels > 5:
            other_half(4, part)
            own_half(5, part)

    def share_five(slot):
        if levels > 4:
            for part in range(2):
                quarter_copy(4, part, slot).wait_recv()
                quarter_share(4, part, slot).start()

    def relay(part):
        mate_copy(part, 0).wait_recv()

        @pl.when(gives)
        def _():
            if part == 0:
                hop_mod().start()
            hop_copy(part).start()

    parts = 2

    def first_part(i):
        every_head(first, heads * i // parts, heads * (i + 1) // parts)

    first_part(0)
    greet(1)
    first_part(1)
    both(pair_three)
    greet(2)
    share_three(0)
    greet(3)
    both(share_two)
    both(lambda part: mate_copy(part, 1).start())
    for b in range(4, levels + 1):
        greet(b)
    share_three(1)
    mod_copy().wait_recv()
    relay(0)
    coarse_mate(0, 0)
    relay(1)
    coarse_mate(1, 0)
    near_bias(1, mate_mod[1])
    for slot in range(2):
        both(lambda part: quarter_share(2, part, slot).wait_recv())
    every_head(lambda h: update(h, everything, [level_rows(2)]))
    both(two_ready)
    both(four_ready)
    every_head(lambda h: update(h, everything, [level_rows(1), level_rows(3)]))
    share_five(0)
    share_five(1)

    @pl.when(takes)
    def _():
        hop_mod().wait_recv()
        hop_copy(0).wait_recv()

    near_bias(0, cross_mod[...])
    last = []
    if levels > 4:
        for slot in range(2):
            both(lambda part: quarter_share(4, part, slot).wait_recv())
        last.append(level_rows(4))
    for b in range(5, levels):
        for part in range(2):
            other_half(b, part)
            whole_copy(b, part).start()
            whole_copy(b, part).wait_recv()
            if b + 1 < levels:
                own_half(b + 1, part)
        last.append(level_rows(b))
    if last:
        every_head(lambda h: update(h, everything, last))
    mate_copy(0, 1).wait_recv()
    coarse_mate(0, 1)
    every_head(weigh)
    pl.when(takes)(lambda: hop_copy(1).wait_recv())
    mate_copy(1, 1).wait_recv()
    coarse_mate(1, 1)
    every_head(finish)

    @pl.when(gives)
    def _():
        both(lambda part: hop_copy(part).wait_send())
        hop_mod().wait_send()

    mod_copy().wait_send()
    for part in range(2):
        three_copy(part).wait_send()
        for role in range(2):
            mate_copy(part, role).wait_send()
        half_copy(1, part).wait_send()
        share_copy(1, part).wait_send()
        whole_copy(3, part).wait_send()
        for b in (2, 4):
            for slot in range(2):
                if b < levels:
                    quarter_copy(b, part, slot).wait_send()
                    quarter_share(b, part, slot).wait_send()
        for b in range(5, levels):
            whole_copy(b, part).wait_send()


def shards(levels, inner, queries, keys, values, modality):
    rows, width = queries.shape
    heads = width // HEAD_DIM
    labels = modality.reshape(rows // BLOCK, 1, BLOCK)
    hbm = pl.BlockSpec(memory_space=pl.ANY)
    state = pltpu.VMEM((heads, rows, HEAD_DIM), F32)
    shard = pltpu.VMEM((rows, width), BF16)
    level = pltpu.VMEM((levels, 2, BLOCK, width), BF16)
    label = pltpu.VMEM((rows // BLOCK, 1, BLOCK), jnp.int32)
    return pl.pallas_call(
        functools.partial(kernel, levels, inner),
        out_shape=pltpu.VMEM((rows, width), BF16),
        in_specs=[hbm] * 4,
        out_specs=pl.BlockSpec(memory_space=pltpu.VMEM),
        scratch_shapes=[
            shard,
            shard,
            shard,
            label,
            level,
            level,
            pltpu.VMEM((2, rows, width), BF16),
            label,
            pltpu.VMEM((2, BLOCK, width), BF16),
            pltpu.VMEM((1, BLOCK), jnp.int32),
            pltpu.VMEM((rows, 2 * BLOCK), F32),
            pltpu.VMEM((rows, BLOCK), F32),
            state,
            state,
            state,
            pltpu.VMEM((heads, rows, 2 * BLOCK), BF16),
            pltpu.VMEM((heads, rows, BLOCK), BF16),
            pltpu.SemaphoreType.REGULAR((levels,)),
            pltpu.SemaphoreType.DMA((4, 2)),
            pltpu.SemaphoreType.DMA((levels, 2, 4)),
            pltpu.SemaphoreType.DMA((levels, 2, 4)),
            pltpu.SemaphoreType.DMA((3, 3)),
            pltpu.SemaphoreType.DMA((3, 3)),
            pltpu.SemaphoreType.DMA((3,)),
            pltpu.SemaphoreType.DMA((3,)),
        ],
        compiler_params=pltpu.CompilerParams(
            collective_id=0, has_side_effects=True, vmem_limit_bytes=56 * 2**20
        ),
    )(queries, keys, values, labels)


def solution(mesh):
    outer, inner = mesh.shape["outer"], mesh.shape["inner"]
    levels = (outer * inner).bit_length() - 1
    rows = P(AXES, None)
    return jax.shard_map(
        functools.partial(shards, levels, inner),
        mesh=mesh,
        in_specs=(rows, rows, rows, P(AXES)),
        out_specs=rows,
        check_vma=False,
    )
```

```python
import functools
import math

import jax
import jax.numpy as jnp
from jax import lax
from jax.experimental import pallas as pl
from jax.experimental.pallas import tpu as pltpu
from jax.sharding import PartitionSpec as P

HEAD_DIM = 128
BLOCK = 128
AXES = ("outer", "inner")
MESH = pl.DeviceIdType.MESH
F32 = jnp.float32
BF16 = jnp.bfloat16


def pair_means(rows):
    half = rows.shape[0] // 2
    r = lax.broadcasted_iota(jnp.int32, (half, rows.shape[0]), 0)
    c = lax.broadcasted_iota(jnp.int32, (half, rows.shape[0]), 1)
    mix = jnp.where(c // 2 == r, 0.5, 0.0).astype(BF16)
    return jnp.dot(mix, rows, preferred_element_type=F32).astype(BF16)


def kernel(
    levels, inner, q_hbm, k_hbm, v_hbm, mod_hbm, out_ref,
    q_ref, k_ref, v_ref, mod_ref, node, far, mate, mate_mod, cross, cross_mod,
    bias_own, bias_near, m_ref, l_ref, acc_ref, p_near, p_coarse,
    ready, load_sem, far_send, far_recv, mate_send, mate_recv, cross_send, cross_recv,
):
    rows, width = q_ref.shape
    heads = width // HEAD_DIM
    half = BLOCK // 2
    quarter = BLOCK // 4
    count = 2**levels
    me = lax.axis_index("outer") * inner + lax.axis_index("inner")
    scale = HEAD_DIM**-0.5 * math.log2(math.e)
    own = (k_ref, v_ref)

    def place(d):
        return (d // inner, d % inner)

    def bit(b):
        return me // 2**b % 2

    def flip(b):
        return me + 2**b * (1 - 2 * bit(b))

    odd = bit(0)
    hop_out = jnp.where(odd == 0, (me + 2) % count, (me + count - 2) % count)
    gives = ((odd == 0) & (me + 2 < count)) | ((odd == 1) & (me > 2))
    takes = ((odd == 0) & (me > 0)) | ((odd == 1) & (me + 1 < count))

    barrier = pltpu.get_barrier_semaphore()
    for b in range(levels):
        pl.semaphore_signal(barrier, inc=1, device_id=place(flip(b)), device_id_type=MESH)

    def span(start, size):
        return pl.ds(pl.multiple_of(start, size), size)

    def block_rows(i):
        return span(i * BLOCK, BLOCK)

    def load(i, role):
        block = odd if role == 0 else 1 - odd
        src, dst = ((k_hbm, k_ref), (v_hbm, v_ref), (mod_hbm, mod_ref), (q_hbm, q_ref))[i]
        if i == 2:
            src, dst = src.at[block], dst.at[role]
        else:
            src, dst = src.at[block_rows(block)], dst.at[pl.ds(role * BLOCK, BLOCK)]
        return pltpu.make_async_copy(src, dst, load_sem.at[i, role])

    def loaded(i):
        load(i, 0).wait()
        load(i, 1).wait()

    for i in range(4):
        load(i, 0).start()
        load(i, 1).start()

    def half_rows(upper):
        return span(upper * half, half)

    def quarter_rows(upper, lower):
        return span(upper * half + lower * quarter, quarter)

    def own_half(b, part):
        node[b, part, half_rows(bit(b - 1)), :] = pair_means(node[b - 1, part])

    def other_half(b, part):
        node[b, part, half_rows(1 - bit(b - 1)), :] = pair_means(far[b - 1, part])

    for part in range(2):
        loaded(part)
        two = pair_means(pair_means(own[part][...]))
        node[1, part, half_rows(odd), :] = two
        node[2, part, quarter_rows(bit(1), odd), :] = pair_means(two)

    @pl.when(~takes)
    def _():
        cross[...] = jnp.zeros(cross.shape, BF16)
        cross_mod[...] = jnp.full(cross_mod.shape, -1, jnp.int32)

    pl.semaphore_wait(barrier, levels)

    def greet(b):
        if b > 0:
            pl.semaphore_wait(ready.at[b - 1], 1)
        if b < levels:
            pl.semaphore_signal(ready.at[b], inc=1, device_id=place(flip(b)), device_id_type=MESH)

    def remote(src, dst, send, recv, target):
        return pltpu.make_async_remote_copy(
            src_ref=src, dst_ref=dst, send_sem=send, recv_sem=recv,
            device_id=place(target), device_id_type=MESH,
        )

    def level_copy(b, part, slot, view, target, src=None):
        src = node if src is None else src
        return remote(src.at[b, part, view], far.at[b, part, view],
                      far_send.at[b, part, slot], far_recv.at[b, part, slot], target)

    def whole_copy(b, part):
        return level_copy(b, part, 0, pl.ds(0, BLOCK), flip(b))

    def half_copy(b, part):
        return level_copy(b, part, 0, half_rows(bit(b - 1)), flip(b))

    def share_copy(b, part):
        return level_copy(b, part, 1, half_rows(bit(b - 1)), flip(b - 1), far)

    def five_view(slot):
        return quarter_rows(bit(3), bit(2) if slot == 0 else 1 - bit(2))

    def piece_view(b, slot):
        return quarter_rows(bit(1), odd if slot == 0 else 1 - odd) if b == 2 else five_view(slot)

    def piece_copy(b, part, slot):
        return level_copy(b, part, slot, piece_view(b, slot), flip(b))

    def piece_share(b, part, slot):
        return level_copy(b, part, 2 + slot, piece_view(b, slot), flip(b - 1), far)

    def three_copy(part):
        view = node.at[2, part, piece_view(2, 0)]
        return remote(view, view, mate_send.at[part, 2], mate_recv.at[part, 2], flip(0))

    def mate_copy(part, role):
        view = pl.ds(role * BLOCK, BLOCK)
        return remote(own[part].at[view], mate.at[part, view],
                      mate_send.at[part, role], mate_recv.at[part, role], flip(0))

    def mod_copy():
        return remote(mod_ref, mate_mod, mate_send.at[2, 0], mate_recv.at[2, 0], flip(0))

    def hop_copy(part):
        return remote(mate.at[part, pl.ds(0, BLOCK)], cross.at[part],
                      cross_send.at[part], cross_recv.at[part], hop_out)

    def hop_mod():
        return remote(mate_mod.at[0], cross_mod, cross_send.at[2], cross_recv.at[2], hop_out)

    loaded(2)
    for part in range(2):
        three_copy(part).start()
    for part in range(2):
        piece_copy(2, part, 0).start()
    for part in range(2):
        half_copy(1, part).start()
    mod_copy().start()
    for part in range(2):
        mate_copy(part, 0).start()
    greet(0)
    loaded(3)

    def label_rows(i):
        return jnp.broadcast_to(mod_ref[i].astype(F32), (BLOCK, BLOCK))

    labels = [label_rows(0), label_rows(1)]
    columns = [jnp.transpose(x) for x in labels]
    zero = jnp.zeros((BLOCK, BLOCK), F32)
    for i in range(2):
        for j in range(2):
            value = zero if i == j else jnp.where(labels[j] == columns[i], 0.0, -jnp.inf)
            bias_own[i * BLOCK : (i + 1) * BLOCK, j * BLOCK : (j + 1) * BLOCK] = value

    def head_cols(h):
        return pl.ds(pl.multiple_of(h * HEAD_DIM, HEAD_DIM), HEAD_DIM)

    def score(q, k):
        return lax.dot_general(q, k, (((1,), (1,)), ((), ())), preferred_element_type=F32) * scale

    def first(h):
        cols = head_cols(h)
        s = score(q_ref[:, cols], k_ref[:, cols]) + bias_own[...]
        m = jnp.broadcast_to(jnp.max(s, axis=1, keepdims=True), (rows, BLOCK))
        p0 = jnp.exp2(s[:, :BLOCK] - m)
        p1 = jnp.exp2(s[:, BLOCK:] - m)
        m_ref[h] = m
        l_ref[h] = p0 + p1
        p = jnp.concatenate([p0.astype(BF16), p1.astype(BF16)], axis=1)
        acc_ref[h] = jnp.dot(p, v_ref[:, cols], preferred_element_type=F32)

    def merged(h, view, sources):
        cols = head_cols(h)
        q = q_ref[view, cols]
        scores = []
        for k, v in sources:
            scores.append(score(q, k[:, cols]))
        best = functools.reduce(jnp.maximum, scores)
        m_old = m_ref[h, view]
        m = jnp.maximum(m_old, jnp.max(best, axis=1, keepdims=True))
        a = jnp.exp2(m_old - m)
        weights = [jnp.exp2(s - m) for s in scores]
        l = l_ref[h, view] * a + functools.reduce(jnp.add, weights)
        p = jnp.concatenate([w.astype(BF16) for w in weights], axis=1)
        rows_in = jnp.concatenate([v[:, cols] for k, v in sources], axis=0)
        acc = acc_ref[h, view] * a + jnp.dot(p, rows_in, preferred_element_type=F32)
        return m, l, acc

    def update(h, view, sources):
        m, l, acc = merged(h, view, sources)
        m_ref[h, view] = m
        l_ref[h, view] = l
        acc_ref[h, view] = acc

    def weigh(h):
        cols = head_cols(h)
        q = q_ref[:, cols]
        s = score(q, jnp.concatenate([cross[0, :, cols], mate[0, BLOCK:rows, cols]], axis=0))
        near = jnp.concatenate([s[:BLOCK, :BLOCK], s[BLOCK:, BLOCK:]], axis=0) + bias_near[...]
        coarse = score(q, far[0, 0, :, cols])
        m_old = m_ref[h]
        m = jnp.maximum(m_old, jnp.max(jnp.maximum(near, coarse), axis=1, keepdims=True))
        a = jnp.exp2(m_old - m)
        near = jnp.exp2(near - m)
        coarse = jnp.exp2(coarse - m)
        total = jnp.sum(l_ref[h] * a + near + coarse, axis=1, keepdims=True)
        l_ref[h] = jnp.broadcast_to(1.0 / total, (rows, HEAD_DIM))
        acc_ref[h] = acc_ref[h] * a
        near = near.astype(BF16)
        none = jnp.zeros((BLOCK, BLOCK), BF16)
        p_near[h, 0:BLOCK, :] = jnp.concatenate([near[:BLOCK], none], axis=1)
        p_near[h, BLOCK:rows, :] = jnp.concatenate([none, near[BLOCK:]], axis=1)
        p_coarse[h] = coarse.astype(BF16)

    def finish(h):
        cols = head_cols(h)
        beside = jnp.concatenate([cross[1, :, cols], mate[1, BLOCK:rows, cols]], axis=0)
        acc = acc_ref[h] + jnp.dot(p_near[h], beside, preferred_element_type=F32)
        acc = acc + jnp.dot(p_coarse[h], far[0, 1, :, cols], preferred_element_type=F32)
        acc = acc * l_ref[h]
        one, two = acc[:BLOCK], acc[BLOCK:]
        out_ref[0:BLOCK, cols] = jnp.where(odd == 0, one, two).astype(BF16)
        out_ref[BLOCK:rows, cols] = jnp.where(odd == 0, two, one).astype(BF16)

    def every_head(body, low=0, high=heads):
        def step(h, carry):
            body(h)
            return carry

        lax.fori_loop(low, high, step, 0, unroll=8)

    everything = pl.ds(0, rows)

    def near_bias(role, label):
        other = jnp.broadcast_to(label.astype(F32), (BLOCK, BLOCK))
        mine = jnp.transpose(label_rows(role))
        bias_near[role * BLOCK : (role + 1) * BLOCK, :] = jnp.where(other == mine, 0.0, -jnp.inf)

    def level_rows(b):
        return (far.at[b, 0], far.at[b, 1])

    def both(action):
        for part in range(2):
            action(part)

    def coarse_mate(part, role):
        far[0, part, role * half : (role + 1) * half, :] = pair_means(
            mate[part, role * BLOCK : (role + 1) * BLOCK, :]
        )

    def pair_three(part):
        three_copy(part).wait_recv()
        piece_copy(2, part, 1).start()

    def share_two(part):
        half_copy(1, part).wait_recv()
        share_copy(1, part).start()

    def share_three(part, slot):
        piece_copy(2, part, slot).wait_recv()
        piece_share(2, part, slot).start()

    def send_five(part, slot):
        if levels > 4:
            half_of = half_rows(bit(2) if slot == 0 else 1 - bit(2))
            node[4, part, five_view(slot), :] = pair_means(node[3, part, half_of, :])
            piece_copy(4, part, slot).start()

    def two_ready(part):
        share_copy(1, part).wait_recv()
        other_half(2, part)
        own_half(3, part)
        send_five(part, 0)

    def three_ready(part):
        for slot in range(2):
            piece_share(2, part, slot).wait_recv()
        other_half(3, part)
        whole_copy(3, part).start()
        send_five(part, 1)

    def four_ready(part):
        whole_copy(3, part).wait_recv()
        if levels > 5:
            other_half(4, part)
            own_half(5, part)

    def share_five(slot):
        if levels > 4:
            for part in range(2):
                piece_copy(4, part, slot).wait_recv()
                piece_share(4, part, slot).start()

    def relay(part):
        mate_copy(part, 0).wait_recv()

        @pl.when(gives)
        def _():
            if part == 0:
                hop_mod().start()
            hop_copy(part).start()

    parts = 2

    def first_part(i):
        every_head(first, heads * i // parts, heads * (i + 1) // parts)

    first_part(0)
    greet(1)
    both(pair_three)
    greet(2)
    first_part(1)
    both(lambda part: share_three(part, 0))
    greet(3)
    both(share_two)
    both(lambda part: mate_copy(part, 1).start())
    for b in range(4, levels + 1):
        greet(b)
    mod_copy().wait_recv()
    relay(0)
    coarse_mate(0, 0)
    both(lambda part: share_three(part, 1))
    relay(1)
    coarse_mate(1, 0)
    near_bias(1, mate_mod[1])
    both(two_ready)
    every_head(lambda h: update(h, everything, [level_rows(1)]))
    both(three_ready)
    share_five(0)
    every_head(lambda h: update(h, everything, [level_rows(2)]))
    both(four_ready)
    every_head(lambda h: update(h, everything, [level_rows(3)]))
    share_five(1)

    @pl.when(takes)
    def _():
        hop_mod().wait_recv()
        hop_copy(0).wait_recv()

    near_bias(0, cross_mod[...])
    last = []
    if levels > 4:
        for slot in range(2):
            both(lambda part: piece_share(4, part, slot).wait_recv())
        last.append(level_rows(4))
    for b in range(5, levels):
        for part in range(2):
            other_half(b, part)
            whole_copy(b, part).start()
            whole_copy(b, part).wait_recv()
            if b + 1 < levels:
                own_half(b + 1, part)
        last.append(level_rows(b))
    if last:
        every_head(lambda h: update(h, everything, last))
    mate_copy(0, 1).wait_recv()
    coarse_mate(0, 1)
    every_head(weigh)
    pl.when(takes)(lambda: hop_copy(1).wait_recv())
    mate_copy(1, 1).wait_recv()
    coarse_mate(1, 1)
    every_head(finish)

    @pl.when(gives)
    def _():
        both(lambda part: hop_copy(part).wait_send())
        hop_mod().wait_send()

    mod_copy().wait_send()
    for part in range(2):
        three_copy(part).wait_send()
        for role in range(2):
            mate_copy(part, role).wait_send()
        half_copy(1, part).wait_send()
        share_copy(1, part).wait_send()
        whole_copy(3, part).wait_send()
        for b in (2, 4):
            for slot in range(2):
                if b < levels:
                    piece_copy(b, part, slot).wait_send()
                    piece_share(b, part, slot).wait_send()
        for b in range(5, levels):
            whole_copy(b, part).wait_send()


def shards(levels, inner, queries, keys, values, modality):
    rows, width = queries.shape
    heads = width // HEAD_DIM
    labels = modality.reshape(rows // BLOCK, 1, BLOCK)
    hbm = pl.BlockSpec(memory_space=pl.ANY)
    state = pltpu.VMEM((heads, rows, HEAD_DIM), F32)
    shard = pltpu.VMEM((rows, width), BF16)
    level = pltpu.VMEM((levels, 2, BLOCK, width), BF16)
    label = pltpu.VMEM((rows // BLOCK, 1, BLOCK), jnp.int32)
    return pl.pallas_call(
        functools.partial(kernel, levels, inner),
        out_shape=pltpu.VMEM((rows, width), BF16),
        in_specs=[hbm] * 4,
        out_specs=pl.BlockSpec(memory_space=pltpu.VMEM),
        scratch_shapes=[
            shard,
            shard,
            shard,
            label,
            level,
            level,
            pltpu.VMEM((2, rows, width), BF16),
            label,
            pltpu.VMEM((2, BLOCK, width), BF16),
            pltpu.VMEM((1, BLOCK), jnp.int32),
            pltpu.VMEM((rows, 2 * BLOCK), F32),
            pltpu.VMEM((rows, BLOCK), F32),
            state,
            state,
            state,
            pltpu.VMEM((heads, rows, 2 * BLOCK), BF16),
            pltpu.VMEM((heads, rows, BLOCK), BF16),
            pltpu.SemaphoreType.REGULAR((levels,)),
            pltpu.SemaphoreType.DMA((4, 2)),
            pltpu.SemaphoreType.DMA((levels, 2, 4)),
            pltpu.SemaphoreType.DMA((levels, 2, 4)),
            pltpu.SemaphoreType.DMA((3, 3)),
            pltpu.SemaphoreType.DMA((3, 3)),
            pltpu.SemaphoreType.DMA((3,)),
            pltpu.SemaphoreType.DMA((3,)),
        ],
        compiler_params=pltpu.CompilerParams(
            collective_id=0, has_side_effects=True, vmem_limit_bytes=56 * 2**20
        ),
    )(queries, keys, values, labels)


def solution(mesh):
    outer, inner = mesh.shape["outer"], mesh.shape["inner"]
    levels = (outer * inner).bit_length() - 1
    rows = P(AXES, None)
    return jax.shard_map(
        functools.partial(shards, levels, inner),
        mesh=mesh,
        in_specs=(rows, rows, rows, P(AXES)),
        out_specs=rows,
        check_vma=False,
    )
```

```python
import functools
import math

import jax
import jax.numpy as jnp
from jax import lax
from jax.experimental import pallas as pl
from jax.experimental.pallas import tpu as pltpu
from jax.sharding import PartitionSpec as P

HEAD_DIM = 128
BLOCK = 128
AXES = ("outer", "inner")
MESH = pl.DeviceIdType.MESH
F32 = jnp.float32
BF16 = jnp.bfloat16


def pair_means(rows):
    half = rows.shape[0] // 2
    r = lax.broadcasted_iota(jnp.int32, (half, rows.shape[0]), 0)
    c = lax.broadcasted_iota(jnp.int32, (half, rows.shape[0]), 1)
    mix = jnp.where(c // 2 == r, 0.5, 0.0).astype(BF16)
    return jnp.dot(mix, rows, preferred_element_type=F32).astype(BF16)


def kernel(
    levels, inner, q_hbm, k_hbm, v_hbm, mod_hbm, out_ref,
    q_ref, k_ref, v_ref, mod_ref, node, far, mate, mate_mod, cross, cross_mod,
    bias_own, bias_near, m_ref, l_ref, acc_ref, p_near, p_coarse,
    ready, load_sem, far_send, far_recv, mate_send, mate_recv, cross_send, cross_recv,
):
    rows, width = q_ref.shape
    heads = width // HEAD_DIM
    half = BLOCK // 2
    quarter = BLOCK // 4
    count = 2**levels
    me = lax.axis_index("outer") * inner + lax.axis_index("inner")
    scale = HEAD_DIM**-0.5 * math.log2(math.e)
    own = (k_ref, v_ref)

    def place(d):
        return (d // inner, d % inner)

    def bit(b):
        return me // 2**b % 2

    def flip(b):
        return me + 2**b * (1 - 2 * bit(b))

    odd = bit(0)
    hop_out = jnp.where(odd == 0, (me + 2) % count, (me + count - 2) % count)
    gives = ((odd == 0) & (me + 2 < count)) | ((odd == 1) & (me > 2))
    takes = ((odd == 0) & (me > 0)) | ((odd == 1) & (me + 1 < count))

    barrier = pltpu.get_barrier_semaphore()
    for b in range(levels):
        if b != 2:
            pl.semaphore_signal(barrier, inc=1, device_id=place(flip(b)), device_id_type=MESH)
    middle = bit(1) != bit(2)
    across = me + 2 * (1 - 2 * bit(1)) + 4 * (1 - 2 * bit(2))

    @pl.when(middle)
    def _():
        pl.semaphore_signal(barrier, inc=1, device_id=place(across), device_id_type=MESH)


    def both(action):
        for part in range(2):
            action(part)

    def span(start, size):
        return pl.ds(pl.multiple_of(start, size), size)

    def block_rows(i):
        return span(i * BLOCK, BLOCK)

    def load(i, role):
        block = odd if role == 0 else 1 - odd
        src, dst = ((k_hbm, k_ref), (v_hbm, v_ref), (mod_hbm, mod_ref), (q_hbm, q_ref))[i]
        if i == 2:
            src, dst = src.at[block], dst.at[role]
        else:
            src, dst = src.at[block_rows(block)], dst.at[pl.ds(role * BLOCK, BLOCK)]
        return pltpu.make_async_copy(src, dst, load_sem.at[i, role])

    def loaded(i):
        load(i, 0).wait()
        load(i, 1).wait()

    for i in range(4):
        load(i, 0).start()
        load(i, 1).start()

    def half_rows(upper):
        return span(upper * half, half)

    def quarter_rows(upper, lower):
        return span(upper * half + lower * quarter, quarter)

    def own_half(b, part):
        node[b, part, half_rows(bit(b - 1)), :] = pair_means(node[b - 1, part])

    def other_half(b, part):
        node[b, part, half_rows(1 - bit(b - 1)), :] = pair_means(far[b - 1, part])

    for part in range(2):
        loaded(part)
        two = pair_means(pair_means(own[part][...]))
        node[1, part, half_rows(odd), :] = two
        node[2, part, quarter_rows(bit(1), odd), :] = pair_means(two)

    @pl.when(~takes)
    def _():
        cross[...] = jnp.zeros(cross.shape, BF16)
        cross_mod[...] = jnp.full(cross_mod.shape, -1, jnp.int32)

    pl.semaphore_wait(barrier, jnp.where(middle, levels, levels - 1))

    @pl.when(middle)
    def _():
        for target in (flip(1), across):
            pl.semaphore_signal(ready.at[levels], inc=1, device_id=place(target), device_id_type=MESH)

    def greet(b):
        if b > 0:
            pl.semaphore_wait(ready.at[b - 1], 1)
        if b < levels:
            pl.semaphore_signal(ready.at[b], inc=1, device_id=place(flip(b)), device_id_type=MESH)

    def remote(src, dst, send, recv, target):
        return pltpu.make_async_remote_copy(
            src_ref=src, dst_ref=dst, send_sem=send, recv_sem=recv,
            device_id=place(target), device_id_type=MESH,
        )

    def level_copy(b, part, slot, view, target, src=None):
        src = node if src is None else src
        return remote(src.at[b, part, view], far.at[b, part, view],
                      far_send.at[b, part, slot], far_recv.at[b, part, slot], target)

    def whole_copy(b, part):
        return level_copy(b, part, 0, pl.ds(0, BLOCK), flip(b))

    def half_copy(b, part, slot):
        start, size = (0, half // 4) if slot == 0 else (half // 4, half - half // 4)
        view = pl.ds(pl.multiple_of(bit(b - 1) * half + start, half // 4), size)
        return level_copy(b, part, 2 * slot, view, flip(b))

    def share_copy(b, part):
        return level_copy(b, part, 1, half_rows(bit(b - 1)), flip(b - 1), far)

    def five_view(slot):
        return quarter_rows(bit(3), bit(2) if slot == 0 else 1 - bit(2))

    def piece_view(b, slot):
        return quarter_rows(bit(1), odd if slot == 0 else 1 - odd) if b == 2 else five_view(slot)

    def piece_copy(b, part, slot):
        return level_copy(b, part, slot, piece_view(b, slot), flip(b))

    def piece_share(b, part, slot):
        return level_copy(b, part, 2 + slot, piece_view(b, slot), flip(b - 1), far)

    def three_copy(part):
        view = node.at[2, part, piece_view(2, 0)]
        return remote(view, view, mate_send.at[part, 2], mate_recv.at[part, 2], flip(0))

    def mate_copy(part, role):
        view = pl.ds(role * BLOCK, BLOCK)
        return remote(own[part].at[view], mate.at[part, view],
                      mate_send.at[part, role], mate_recv.at[part, role], flip(0))

    def mod_copy():
        return remote(mod_ref, mate_mod, mate_send.at[2, 0], mate_recv.at[2, 0], flip(0))

    def hop_copy(part):
        return remote(mate.at[part, pl.ds(0, BLOCK)], cross.at[part],
                      cross_send.at[part], cross_recv.at[part], hop_out)

    def hop_mod():
        return remote(mate_mod.at[0], cross_mod, cross_send.at[2], cross_recv.at[2], hop_out)

    loaded(2)
    for part in range(2):
        three_copy(part).start()
    both(lambda part: half_copy(1, part, 0).start())
    mod_copy().start()
    for part in range(2):
        mate_copy(part, 0).start()
    greet(0)
    pl.semaphore_wait(ready.at[levels], 1)
    for part in range(2):
        piece_copy(2, part, 0).start()
    both(lambda part: half_copy(1, part, 1).start())
    loaded(3)

    def label_rows(i):
        return jnp.broadcast_to(mod_ref[i].astype(F32), (BLOCK, BLOCK))

    labels = [label_rows(0), label_rows(1)]
    columns = [jnp.transpose(x) for x in labels]
    zero = jnp.zeros((BLOCK, BLOCK), F32)
    for i in range(2):
        for j in range(2):
            value = zero if i == j else jnp.where(labels[j] == columns[i], 0.0, -jnp.inf)
            bias_own[i * BLOCK : (i + 1) * BLOCK, j * BLOCK : (j + 1) * BLOCK] = value

    def head_cols(h):
        return pl.ds(pl.multiple_of(h * HEAD_DIM, HEAD_DIM), HEAD_DIM)

    def score(q, k):
        return lax.dot_general(q, k, (((1,), (1,)), ((), ())), preferred_element_type=F32) * scale

    def first(h):
        cols = head_cols(h)
        s = score(q_ref[:, cols], k_ref[:, cols]) + bias_own[...]
        m = jnp.broadcast_to(jnp.max(s, axis=1, keepdims=True), (rows, BLOCK))
        p0 = jnp.exp2(s[:, :BLOCK] - m)
        p1 = jnp.exp2(s[:, BLOCK:] - m)
        m_ref[h] = m
        l_ref[h] = p0 + p1
        p = jnp.concatenate([p0.astype(BF16), p1.astype(BF16)], axis=1)
        acc_ref[h] = jnp.dot(p, v_ref[:, cols], preferred_element_type=F32)

    def merged(h, view, sources):
        cols = head_cols(h)
        q = q_ref[view, cols]
        scores = []
        for k, v in sources:
            scores.append(score(q, k[:, cols]))
        best = functools.reduce(jnp.maximum, scores)
        m_old = m_ref[h, view]
        m = jnp.maximum(m_old, jnp.max(best, axis=1, keepdims=True))
        a = jnp.exp2(m_old - m)
        weights = [jnp.exp2(s - m) for s in scores]
        l = l_ref[h, view] * a + functools.reduce(jnp.add, weights)
        p = jnp.concatenate([w.astype(BF16) for w in weights], axis=1)
        rows_in = jnp.concatenate([v[:, cols] for k, v in sources], axis=0)
        acc = acc_ref[h, view] * a + jnp.dot(p, rows_in, preferred_element_type=F32)
        return m, l, acc

    def update(h, view, sources):
        m, l, acc = merged(h, view, sources)
        m_ref[h, view] = m
        l_ref[h, view] = l
        acc_ref[h, view] = acc

    def weigh(h):
        cols = head_cols(h)
        q = q_ref[:, cols]
        s = score(q, jnp.concatenate([cross[0, :, cols], mate[0, BLOCK:rows, cols]], axis=0))
        near = jnp.concatenate([s[:BLOCK, :BLOCK], s[BLOCK:, BLOCK:]], axis=0) + bias_near[...]
        coarse = score(q, far[0, 0, :, cols])
        m_old = m_ref[h]
        m = jnp.maximum(m_old, jnp.max(jnp.maximum(near, coarse), axis=1, keepdims=True))
        a = jnp.exp2(m_old - m)
        near = jnp.exp2(near - m)
        coarse = jnp.exp2(coarse - m)
        total = jnp.sum(l_ref[h] * a + near + coarse, axis=1, keepdims=True)
        l_ref[h] = jnp.broadcast_to(1.0 / total, (rows, HEAD_DIM))
        acc_ref[h] = acc_ref[h] * a
        near = near.astype(BF16)
        none = jnp.zeros((BLOCK, BLOCK), BF16)
        p_near[h, 0:BLOCK, :] = jnp.concatenate([near[:BLOCK], none], axis=1)
        p_near[h, BLOCK:rows, :] = jnp.concatenate([none, near[BLOCK:]], axis=1)
        p_coarse[h] = coarse.astype(BF16)

    def finish(h):
        cols = head_cols(h)
        beside = jnp.concatenate([cross[1, :, cols], mate[1, BLOCK:rows, cols]], axis=0)
        acc = acc_ref[h] + jnp.dot(p_near[h], beside, preferred_element_type=F32)
        acc = acc + jnp.dot(p_coarse[h], far[0, 1, :, cols], preferred_element_type=F32)
        acc = acc * l_ref[h]
        one, two = acc[:BLOCK], acc[BLOCK:]
        out_ref[0:BLOCK, cols] = jnp.where(odd == 0, one, two).astype(BF16)
        out_ref[BLOCK:rows, cols] = jnp.where(odd == 0, two, one).astype(BF16)

    def every_head(body, low=0, high=heads):
        def step(h, carry):
            body(h)
            return carry

        lax.fori_loop(low, high, step, 0, unroll=8)

    everything = pl.ds(0, rows)

    def near_bias(role, label):
        other = jnp.broadcast_to(label.astype(F32), (BLOCK, BLOCK))
        mine = jnp.transpose(label_rows(role))
        bias_near[role * BLOCK : (role + 1) * BLOCK, :] = jnp.where(other == mine, 0.0, -jnp.inf)

    def level_rows(b):
        return (far.at[b, 0], far.at[b, 1])

    def coarse_mate(part, role):
        far[0, part, role * half : (role + 1) * half, :] = pair_means(
            mate[part, role * BLOCK : (role + 1) * BLOCK, :]
        )

    def pair_three(part):
        three_copy(part).wait_recv()
        piece_copy(2, part, 1).start()

    def share_two(part):
        half_copy(1, part, 0).wait_recv()
        half_copy(1, part, 1).wait_recv()
        share_copy(1, part).start()

    def share_three(part, slot):
        piece_copy(2, part, slot).wait_recv()
        piece_share(2, part, slot).start()

    def send_five(part, slot):
        if levels > 4:
            half_of = half_rows(bit(2) if slot == 0 else 1 - bit(2))
            node[4, part, five_view(slot), :] = pair_means(node[3, part, half_of, :])
            piece_copy(4, part, slot).start()

    def two_ready(part):
        share_copy(1, part).wait_recv()
        other_half(2, part)
        own_half(3, part)
        send_five(part, 0)

    def three_ready(part):
        for slot in range(2):
            piece_share(2, part, slot).wait_recv()
        other_half(3, part)
        whole_copy(3, part).start()
        send_five(part, 1)

    def four_ready(part):
        whole_copy(3, part).wait_recv()
        if levels > 5:
            other_half(4, part)
            own_half(5, part)

    def share_five(slot):
        if levels > 4:
            for part in range(2):
                piece_copy(4, part, slot).wait_recv()
                piece_share(4, part, slot).start()

    def relay(part):
        mate_copy(part, 0).wait_recv()

        @pl.when(gives)
        def _():
            if part == 0:
                hop_mod().start()
            hop_copy(part).start()

    parts = 2

    def first_part(i):
        every_head(first, heads * i // parts, heads * (i + 1) // parts)

    first_part(0)
    greet(1)
    both(pair_three)
    greet(2)
    first_part(1)
    both(lambda part: share_three(part, 0))
    greet(3)
    both(share_two)
    both(lambda part: mate_copy(part, 1).start())
    for b in range(4, levels + 1):
        greet(b)
    mod_copy().wait_recv()
    relay(0)
    coarse_mate(0, 0)
    both(lambda part: share_three(part, 1))
    relay(1)
    coarse_mate(1, 0)
    near_bias(1, mate_mod[1])
    both(two_ready)
    every_head(lambda h: update(h, everything, [level_rows(1)]))
    both(three_ready)
    share_five(0)
    every_head(lambda h: update(h, everything, [level_rows(2)]))
    both(four_ready)
    every_head(lambda h: update(h, everything, [level_rows(3)]))
    share_five(1)

    @pl.when(takes)
    def _():
        hop_mod().wait_recv()
        hop_copy(0).wait_recv()

    near_bias(0, cross_mod[...])
    last = []
    if levels > 4:
        for slot in range(2):
            both(lambda part: piece_share(4, part, slot).wait_recv())
        last.append(level_rows(4))
    for b in range(5, levels):
        for part in range(2):
            other_half(b, part)
            whole_copy(b, part).start()
            whole_copy(b, part).wait_recv()
            if b + 1 < levels:
                own_half(b + 1, part)
        last.append(level_rows(b))
    if last:
        every_head(lambda h: update(h, everything, last))
    mate_copy(0, 1).wait_recv()
    coarse_mate(0, 1)
    every_head(weigh)
    pl.when(takes)(lambda: hop_copy(1).wait_recv())
    mate_copy(1, 1).wait_recv()
    coarse_mate(1, 1)
    every_head(finish)

    @pl.when(gives)
    def _():
        both(lambda part: hop_copy(part).wait_send())
        hop_mod().wait_send()

    mod_copy().wait_send()
    for part in range(2):
        three_copy(part).wait_send()
        for role in range(2):
            mate_copy(part, role).wait_send()
        half_copy(1, part, 0).wait_send()
        half_copy(1, part, 1).wait_send()
        share_copy(1, part).wait_send()
        whole_copy(3, part).wait_send()
        for b in (2, 4):
            for slot in range(2):
                if b < levels:
                    piece_copy(b, part, slot).wait_send()
                    piece_share(b, part, slot).wait_send()
        for b in range(5, levels):
            whole_copy(b, part).wait_send()


def shards(levels, inner, queries, keys, values, modality):
    rows, width = queries.shape
    heads = width // HEAD_DIM
    labels = modality.reshape(rows // BLOCK, 1, BLOCK)
    hbm = pl.BlockSpec(memory_space=pl.ANY)
    state = pltpu.VMEM((heads, rows, HEAD_DIM), F32)
    shard = pltpu.VMEM((rows, width), BF16)
    level = pltpu.VMEM((levels, 2, BLOCK, width), BF16)
    label = pltpu.VMEM((rows // BLOCK, 1, BLOCK), jnp.int32)
    return pl.pallas_call(
        functools.partial(kernel, levels, inner),
        out_shape=pltpu.VMEM((rows, width), BF16),
        in_specs=[hbm] * 4,
        out_specs=pl.BlockSpec(memory_space=pltpu.VMEM),
        scratch_shapes=[
            shard,
            shard,
            shard,
            label,
            level,
            level,
            pltpu.VMEM((2, rows, width), BF16),
            label,
            pltpu.VMEM((2, BLOCK, width), BF16),
            pltpu.VMEM((1, BLOCK), jnp.int32),
            pltpu.VMEM((rows, 2 * BLOCK), F32),
            pltpu.VMEM((rows, BLOCK), F32),
            state,
            state,
            state,
            pltpu.VMEM((heads, rows, 2 * BLOCK), BF16),
            pltpu.VMEM((heads, rows, BLOCK), BF16),
            pltpu.SemaphoreType.REGULAR((levels + 1,)),
            pltpu.SemaphoreType.DMA((4, 2)),
            pltpu.SemaphoreType.DMA((levels, 2, 4)),
            pltpu.SemaphoreType.DMA((levels, 2, 4)),
            pltpu.SemaphoreType.DMA((3, 3)),
            pltpu.SemaphoreType.DMA((3, 3)),
            pltpu.SemaphoreType.DMA((3,)),
            pltpu.SemaphoreType.DMA((3,)),
        ],
        compiler_params=pltpu.CompilerParams(
            collective_id=0, has_side_effects=True, vmem_limit_bytes=56 * 2**20
        ),
    )(queries, keys, values, labels)


def solution(mesh):
    outer, inner = mesh.shape["outer"], mesh.shape["inner"]
    levels = (outer * inner).bit_length() - 1
    rows = P(AXES, None)
    return jax.shard_map(
        functools.partial(shards, levels, inner),
        mesh=mesh,
        in_specs=(rows, rows, rows, P(AXES)),
        out_specs=rows,
        check_vma=False,
    )
```

```python
import functools
import math

import jax
import jax.numpy as jnp
from jax import lax
from jax.experimental import pallas as pl
from jax.experimental.pallas import tpu as pltpu
from jax.sharding import PartitionSpec as P

HEAD_DIM = 128
BLOCK = 128
AXES = ("outer", "inner")
MESH = pl.DeviceIdType.MESH
F32 = jnp.float32
BF16 = jnp.bfloat16


def pair_means(rows):
    half = rows.shape[0] // 2
    r = lax.broadcasted_iota(jnp.int32, (half, rows.shape[0]), 0)
    c = lax.broadcasted_iota(jnp.int32, (half, rows.shape[0]), 1)
    mix = jnp.where(c // 2 == r, 0.5, 0.0).astype(BF16)
    return jnp.dot(mix, rows, preferred_element_type=F32).astype(BF16)


def kernel(
    levels, inner, q_hbm, k_hbm, v_hbm, mod_hbm, out_ref,
    q_ref, k_ref, v_ref, mod_ref, node, far, mate, mate_mod, cross, cross_mod,
    bias_own, bias_near, m_ref, l_ref, acc_ref, p_near, p_coarse,
    ready, load_sem, far_send, far_recv, mate_send, mate_recv, cross_send, cross_recv,
):
    rows, width = q_ref.shape
    heads = width // HEAD_DIM
    half = BLOCK // 2
    quarter = BLOCK // 4
    count = 2**levels
    me = lax.axis_index("outer") * inner + lax.axis_index("inner")
    scale = HEAD_DIM**-0.5 * math.log2(math.e)
    own = (k_ref, v_ref)

    def place(d):
        return (d // inner, d % inner)

    def bit(b):
        return me // 2**b % 2

    def flip(b):
        return me + 2**b * (1 - 2 * bit(b))

    odd = bit(0)
    hop_out = jnp.where(odd == 0, (me + 2) % count, (me + count - 2) % count)
    gives = ((odd == 0) & (me + 2 < count)) | ((odd == 1) & (me > 2))
    takes = ((odd == 0) & (me > 0)) | ((odd == 1) & (me + 1 < count))

    barrier = pltpu.get_barrier_semaphore()
    for b in range(levels):
        if b != 2:
            pl.semaphore_signal(barrier, inc=1, device_id=place(flip(b)), device_id_type=MESH)
    middle = bit(1) != bit(2)
    across = me + 2 * (1 - 2 * bit(1)) + 4 * (1 - 2 * bit(2))

    @pl.when(middle)
    def _():
        pl.semaphore_signal(barrier, inc=1, device_id=place(across), device_id_type=MESH)


    def both(action):
        for part in range(2):
            action(part)

    def span(start, size):
        return pl.ds(pl.multiple_of(start, size), size)

    def block_rows(i):
        return span(i * BLOCK, BLOCK)

    def load(i, role):
        block = odd if role == 0 else 1 - odd
        src, dst = ((k_hbm, k_ref), (v_hbm, v_ref), (mod_hbm, mod_ref), (q_hbm, q_ref))[i]
        if i == 2:
            src, dst = src.at[block], dst.at[role]
        else:
            src, dst = src.at[block_rows(block)], dst.at[pl.ds(role * BLOCK, BLOCK)]
        return pltpu.make_async_copy(src, dst, load_sem.at[i, role])

    def loaded(i):
        load(i, 0).wait()
        load(i, 1).wait()

    for i in range(4):
        load(i, 0).start()
        load(i, 1).start()

    def half_rows(upper):
        return span(upper * half, half)

    def quarter_rows(upper, lower):
        return span(upper * half + lower * quarter, quarter)

    def own_half(b, part):
        node[b, part, half_rows(bit(b - 1)), :] = pair_means(node[b - 1, part])

    def other_half(b, part):
        node[b, part, half_rows(1 - bit(b - 1)), :] = pair_means(far[b - 1, part])

    loaded(0)
    loaded(1)
    ones = [pair_means(own[part][...]) for part in range(2)]
    twos = [pair_means(one) for one in ones]
    threes = [pair_means(two) for two in twos]
    for part in range(2):
        node[1, part, half_rows(odd), :] = twos[part]
        node[2, part, quarter_rows(bit(1), odd), :] = threes[part]

    @pl.when(~takes)
    def _():
        cross[...] = jnp.zeros(cross.shape, BF16)
        cross_mod[...] = jnp.full(cross_mod.shape, -1, jnp.int32)

    pl.semaphore_wait(barrier, jnp.where(middle, levels, levels - 1))

    @pl.when(middle)
    def _():
        for target in (flip(1), across):
            pl.semaphore_signal(ready.at[levels], inc=1, device_id=place(target), device_id_type=MESH)

    def greet(b):
        if b > 0:
            pl.semaphore_wait(ready.at[b - 1], 1)
        if b < levels:
            pl.semaphore_signal(ready.at[b], inc=1, device_id=place(flip(b)), device_id_type=MESH)

    def remote(src, dst, send, recv, target):
        return pltpu.make_async_remote_copy(
            src_ref=src, dst_ref=dst, send_sem=send, recv_sem=recv,
            device_id=place(target), device_id_type=MESH,
        )

    def level_copy(b, part, slot, view, target, src=None):
        src = node if src is None else src
        return remote(src.at[b, part, view], far.at[b, part, view],
                      far_send.at[b, part, slot], far_recv.at[b, part, slot], target)

    def whole_copy(b, part):
        return level_copy(b, part, 0, pl.ds(0, BLOCK), flip(b))

    def half_copy(b, part, slot):
        start, size = (0, half // 4) if slot == 0 else (half // 4, half - half // 4)
        view = pl.ds(pl.multiple_of(bit(b - 1) * half + start, half // 4), size)
        return level_copy(b, part, 2 * slot, view, flip(b))

    def share_copy(b, part):
        return level_copy(b, part, 1, half_rows(bit(b - 1)), flip(b - 1), far)

    def five_view(slot):
        return quarter_rows(bit(3), bit(2) if slot == 0 else 1 - bit(2))

    def piece_view(b, slot):
        return quarter_rows(bit(1), odd if slot == 0 else 1 - odd) if b == 2 else five_view(slot)

    def piece_copy(b, part, slot):
        return level_copy(b, part, slot, piece_view(b, slot), flip(b))

    def piece_share(b, part, slot):
        return level_copy(b, part, 2 + slot, piece_view(b, slot), flip(b - 1), far)

    def three_copy(part):
        view = node.at[2, part, piece_view(2, 0)]
        return remote(view, view, mate_send.at[part, 2], mate_recv.at[part, 2], flip(0))

    def mate_copy(part, role):
        view = pl.ds(role * BLOCK, BLOCK)
        return remote(own[part].at[view], mate.at[part, view],
                      mate_send.at[part, role], mate_recv.at[part, role], flip(0))

    def last_copy(i):
        view = pl.ds(BLOCK + i * half, half)
        return remote(v_ref.at[view], mate.at[1, view],
                      mate_send.at[1 + i, 1], mate_recv.at[1 + i, 1], flip(0))

    def mod_copy():
        return remote(mod_ref, mate_mod, mate_send.at[2, 0], mate_recv.at[2, 0], flip(0))

    def hop_copy(part):
        return remote(mate.at[part, pl.ds(0, BLOCK)], cross.at[part],
                      cross_send.at[part], cross_recv.at[part], hop_out)

    def hop_mod():
        return remote(mate_mod.at[0], cross_mod, cross_send.at[2], cross_recv.at[2], hop_out)

    loaded(2)
    for part in range(2):
        three_copy(part).start()
    both(lambda part: half_copy(1, part, 0).start())
    mod_copy().start()
    for part in range(2):
        mate_copy(part, 0).start()
    greet(0)
    pl.semaphore_wait(ready.at[levels], 1)
    for part in range(2):
        piece_copy(2, part, 0).start()
    both(lambda part: half_copy(1, part, 1).start())
    loaded(3)

    def label_rows(i):
        return jnp.broadcast_to(mod_ref[i].astype(F32), (BLOCK, BLOCK))

    labels = [label_rows(0), label_rows(1)]
    columns = [jnp.transpose(x) for x in labels]
    zero = jnp.zeros((BLOCK, BLOCK), F32)
    for i in range(2):
        for j in range(2):
            value = zero if i == j else jnp.where(labels[j] == columns[i], 0.0, -jnp.inf)
            bias_own[i * BLOCK : (i + 1) * BLOCK, j * BLOCK : (j + 1) * BLOCK] = value

    def head_cols(h):
        return pl.ds(pl.multiple_of(h * HEAD_DIM, HEAD_DIM), HEAD_DIM)

    def score(q, k):
        return lax.dot_general(q, k, (((1,), (1,)), ((), ())), preferred_element_type=F32) * scale

    def first(h):
        cols = head_cols(h)
        s = score(q_ref[:, cols], k_ref[:, cols]) + bias_own[...]
        m = jnp.broadcast_to(jnp.max(s, axis=1, keepdims=True), (rows, BLOCK))
        p0 = jnp.exp2(s[:, :BLOCK] - m)
        p1 = jnp.exp2(s[:, BLOCK:] - m)
        m_ref[h] = m
        l_ref[h] = p0 + p1
        p = jnp.concatenate([p0.astype(BF16), p1.astype(BF16)], axis=1)
        acc_ref[h] = jnp.dot(p, v_ref[:, cols], preferred_element_type=F32)

    def merged(h, view, sources):
        cols = head_cols(h)
        q = q_ref[view, cols]
        scores = []
        for k, v in sources:
            scores.append(score(q, k[:, cols]))
        best = functools.reduce(jnp.maximum, scores)
        m_old = m_ref[h, view]
        m = jnp.maximum(m_old, jnp.max(best, axis=1, keepdims=True))
        a = jnp.exp2(m_old - m)
        weights = [jnp.exp2(s - m) for s in scores]
        l = l_ref[h, view] * a + functools.reduce(jnp.add, weights)
        p = jnp.concatenate([w.astype(BF16) for w in weights], axis=1)
        rows_in = jnp.concatenate([v[:, cols] for k, v in sources], axis=0)
        acc = acc_ref[h, view] * a + jnp.dot(p, rows_in, preferred_element_type=F32)
        return m, l, acc

    def update(h, view, sources):
        m, l, acc = merged(h, view, sources)
        m_ref[h, view] = m
        l_ref[h, view] = l
        acc_ref[h, view] = acc

    def weigh(h):
        cols = head_cols(h)
        q = q_ref[:, cols]
        s = score(q, jnp.concatenate([cross[0, :, cols], mate[0, BLOCK:rows, cols]], axis=0))
        near = jnp.concatenate([s[:BLOCK, :BLOCK], s[BLOCK:, BLOCK:]], axis=0) + bias_near[...]
        coarse = score(q, far[0, 0, :, cols])
        m_old = m_ref[h]
        m = jnp.maximum(m_old, jnp.max(jnp.maximum(near, coarse), axis=1, keepdims=True))
        a = jnp.exp2(m_old - m)
        near = jnp.exp2(near - m)
        coarse = jnp.exp2(coarse - m)
        total = jnp.sum(l_ref[h] * a + near + coarse, axis=1, keepdims=True)
        l_ref[h] = jnp.broadcast_to(1.0 / total, (rows, HEAD_DIM))
        acc_ref[h] = acc_ref[h] * a
        near = near.astype(BF16)
        none = jnp.zeros((BLOCK, BLOCK), BF16)
        p_near[h, 0:BLOCK, :] = jnp.concatenate([near[:BLOCK], none], axis=1)
        p_near[h, BLOCK:rows, :] = jnp.concatenate([none, near[BLOCK:]], axis=1)
        p_coarse[h] = coarse.astype(BF16)

    def finish(h):
        cols = head_cols(h)
        beside = jnp.concatenate([cross[1, :, cols], mate[1, BLOCK:rows, cols]], axis=0)
        acc = acc_ref[h] + jnp.dot(p_near[h], beside, preferred_element_type=F32)
        acc = acc + jnp.dot(p_coarse[h], far[0, 1, :, cols], preferred_element_type=F32)
        acc = acc * l_ref[h]
        one, two = acc[:BLOCK], acc[BLOCK:]
        out_ref[0:BLOCK, cols] = jnp.where(odd == 0, one, two).astype(BF16)
        out_ref[BLOCK:rows, cols] = jnp.where(odd == 0, two, one).astype(BF16)

    def every_head(body, low=0, high=heads):
        def step(h, carry):
            body(h)
            return carry

        lax.fori_loop(low, high, step, 0, unroll=8)

    everything = pl.ds(0, rows)

    def near_bias(role, label):
        other = jnp.broadcast_to(label.astype(F32), (BLOCK, BLOCK))
        mine = jnp.transpose(label_rows(role))
        bias_near[role * BLOCK : (role + 1) * BLOCK, :] = jnp.where(other == mine, 0.0, -jnp.inf)

    def level_rows(b):
        return (far.at[b, 0], far.at[b, 1])

    def coarse_mate(part, role):
        far[0, part, role * half : (role + 1) * half, :] = pair_means(
            mate[part, role * BLOCK : (role + 1) * BLOCK, :]
        )

    def pair_three(part):
        three_copy(part).wait_recv()
        piece_copy(2, part, 1).start()

    def share_two(part):
        half_copy(1, part, 0).wait_recv()
        half_copy(1, part, 1).wait_recv()
        share_copy(1, part).start()

    def share_three(part, slot):
        piece_copy(2, part, slot).wait_recv()
        piece_share(2, part, slot).start()

    def send_five(part, slot):
        if levels > 4:
            half_of = half_rows(bit(2) if slot == 0 else 1 - bit(2))
            node[4, part, five_view(slot), :] = pair_means(node[3, part, half_of, :])
            piece_copy(4, part, slot).start()

    def two_ready(part):
        share_copy(1, part).wait_recv()
        other_half(2, part)
        own_half(3, part)
        send_five(part, 0)

    def three_ready(part):
        for slot in range(2):
            piece_share(2, part, slot).wait_recv()
        other_half(3, part)
        whole_copy(3, part).start()
        send_five(part, 1)

    def four_ready(part):
        whole_copy(3, part).wait_recv()
        if levels > 5:
            other_half(4, part)
            own_half(5, part)

    def share_five(slot):
        if levels > 4:
            for part in range(2):
                piece_copy(4, part, slot).wait_recv()
                piece_share(4, part, slot).start()

    def relay(part):
        mate_copy(part, 0).wait_recv()

        @pl.when(gives)
        def _():
            if part == 0:
                hop_mod().start()
            hop_copy(part).start()

    parts = 2

    def first_part(i):
        every_head(first, heads * i // parts, heads * (i + 1) // parts)

    first_part(0)
    greet(1)
    both(pair_three)
    greet(2)
    first_part(1)
    both(lambda part: share_three(part, 0))
    greet(3)
    both(share_two)
    mate_copy(0, 1).start()
    both(lambda i: last_copy(i).start())
    for b in range(4, levels + 1):
        greet(b)
    mod_copy().wait_recv()
    relay(0)
    coarse_mate(0, 0)
    both(lambda part: share_three(part, 1))
    relay(1)
    coarse_mate(1, 0)
    near_bias(1, mate_mod[1])
    both(two_ready)
    every_head(lambda h: update(h, everything, [level_rows(1)]))
    both(three_ready)
    share_five(0)
    every_head(lambda h: update(h, everything, [level_rows(2)]))
    both(four_ready)
    every_head(lambda h: update(h, everything, [level_rows(3)]))
    share_five(1)

    @pl.when(takes)
    def _():
        hop_mod().wait_recv()
        hop_copy(0).wait_recv()

    near_bias(0, cross_mod[...])
    last = []
    if levels > 4:
        for slot in range(2):
            both(lambda part: piece_share(4, part, slot).wait_recv())
        last.append(level_rows(4))
    for b in range(5, levels):
        for part in range(2):
            other_half(b, part)
            whole_copy(b, part).start()
            whole_copy(b, part).wait_recv()
            if b + 1 < levels:
                own_half(b + 1, part)
        last.append(level_rows(b))
    if last:
        every_head(lambda h: update(h, everything, last))
    mate_copy(0, 1).wait_recv()
    coarse_mate(0, 1)
    every_head(weigh)
    pl.when(takes)(lambda: hop_copy(1).wait_recv())
    for i in range(2):
        last_copy(i).wait_recv()
        far[0, 1, half + i * quarter : half + (i + 1) * quarter, :] = pair_means(
            mate[1, BLOCK + i * half : BLOCK + (i + 1) * half, :]
        )
    every_head(finish)

    @pl.when(gives)
    def _():
        both(lambda part: hop_copy(part).wait_send())
        hop_mod().wait_send()

    mod_copy().wait_send()
    mate_copy(0, 1).wait_send()
    for part in range(2):
        three_copy(part).wait_send()
        mate_copy(part, 0).wait_send()
        last_copy(part).wait_send()
        half_copy(1, part, 0).wait_send()
        half_copy(1, part, 1).wait_send()
        share_copy(1, part).wait_send()
        whole_copy(3, part).wait_send()
        for b in (2, 4):
            for slot in range(2):
                if b < levels:
                    piece_copy(b, part, slot).wait_send()
                    piece_share(b, part, slot).wait_send()
        for b in range(5, levels):
            whole_copy(b, part).wait_send()


def shards(levels, inner, queries, keys, values, modality):
    rows, width = queries.shape
    heads = width // HEAD_DIM
    labels = modality.reshape(rows // BLOCK, 1, BLOCK)
    hbm = pl.BlockSpec(memory_space=pl.ANY)
    state = pltpu.VMEM((heads, rows, HEAD_DIM), F32)
    shard = pltpu.VMEM((rows, width), BF16)
    level = pltpu.VMEM((levels, 2, BLOCK, width), BF16)
    label = pltpu.VMEM((rows // BLOCK, 1, BLOCK), jnp.int32)
    return pl.pallas_call(
        functools.partial(kernel, levels, inner),
        out_shape=pltpu.VMEM((rows, width), BF16),
        in_specs=[hbm] * 4,
        out_specs=pl.BlockSpec(memory_space=pltpu.VMEM),
        scratch_shapes=[
            shard,
            shard,
            shard,
            label,
            level,
            level,
            pltpu.VMEM((2, rows, width), BF16),
            label,
            pltpu.VMEM((2, BLOCK, width), BF16),
            pltpu.VMEM((1, BLOCK), jnp.int32),
            pltpu.VMEM((rows, 2 * BLOCK), F32),
            pltpu.VMEM((rows, BLOCK), F32),
            state,
            state,
            state,
            pltpu.VMEM((heads, rows, 2 * BLOCK), BF16),
            pltpu.VMEM((heads, rows, BLOCK), BF16),
            pltpu.SemaphoreType.REGULAR((levels + 1,)),
            pltpu.SemaphoreType.DMA((4, 2)),
            pltpu.SemaphoreType.DMA((levels, 2, 4)),
            pltpu.SemaphoreType.DMA((levels, 2, 4)),
            pltpu.SemaphoreType.DMA((3, 3)),
            pltpu.SemaphoreType.DMA((3, 3)),
            pltpu.SemaphoreType.DMA((3,)),
            pltpu.SemaphoreType.DMA((3,)),
        ],
        compiler_params=pltpu.CompilerParams(
            collective_id=0, has_side_effects=True, vmem_limit_bytes=56 * 2**20
        ),
    )(queries, keys, values, labels)


def solution(mesh):
    outer, inner = mesh.shape["outer"], mesh.shape["inner"]
    levels = (outer * inner).bit_length() - 1
    rows = P(AXES, None)
    return jax.shard_map(
        functools.partial(shards, levels, inner),
        mesh=mesh,
        in_specs=(rows, rows, rows, P(AXES)),
        out_specs=rows,
        check_vma=False,
    )
```

```python
import functools
import math

import jax
import jax.numpy as jnp
from jax import lax
from jax.experimental import pallas as pl
from jax.experimental.pallas import tpu as pltpu
from jax.sharding import PartitionSpec as P

HEAD_DIM = 128
BLOCK = 128
AXES = ("outer", "inner")
MESH = pl.DeviceIdType.MESH
F32 = jnp.float32
BF16 = jnp.bfloat16


def pair_means(rows):
    half = rows.shape[0] // 2
    r = lax.broadcasted_iota(jnp.int32, (half, rows.shape[0]), 0)
    c = lax.broadcasted_iota(jnp.int32, (half, rows.shape[0]), 1)
    mix = jnp.where(c // 2 == r, 0.5, 0.0).astype(BF16)
    return jnp.dot(mix, rows, preferred_element_type=F32).astype(BF16)


def kernel(
    levels, inner, q_hbm, k_hbm, v_hbm, mod_hbm, out_ref,
    q_ref, k_ref, v_ref, mod_ref, node, far, mate, mate_mod, cross, cross_mod,
    bias_own, bias_near, m_ref, l_ref, acc_ref, p_near, p_coarse,
    ready, load_sem, far_send, far_recv, mate_send, mate_recv, cross_send, cross_recv,
):
    rows, width = q_ref.shape
    heads = width // HEAD_DIM
    half = BLOCK // 2
    quarter = BLOCK // 4
    count = 2**levels
    me = lax.axis_index("outer") * inner + lax.axis_index("inner")
    scale = HEAD_DIM**-0.5 * math.log2(math.e)
    own = (k_ref, v_ref)

    def place(d):
        return (d // inner, d % inner)

    def bit(b):
        return me // 2**b % 2

    def flip(b):
        return me + 2**b * (1 - 2 * bit(b))

    odd = bit(0)
    hop_out = jnp.where(odd == 0, (me + 2) % count, (me + count - 2) % count)
    gives = ((odd == 0) & (me + 2 < count)) | ((odd == 1) & (me > 2))
    takes = ((odd == 0) & (me > 0)) | ((odd == 1) & (me + 1 < count))

    barrier = pltpu.get_barrier_semaphore()
    for b in range(levels):
        if b != 2:
            pl.semaphore_signal(barrier, inc=1, device_id=place(flip(b)), device_id_type=MESH)
    middle = bit(1) != bit(2)
    across = me + 2 * (1 - 2 * bit(1)) + 4 * (1 - 2 * bit(2))

    @pl.when(middle)
    def _():
        pl.semaphore_signal(barrier, inc=1, device_id=place(across), device_id_type=MESH)


    def both(action):
        for part in range(2):
            action(part)

    def span(start, size):
        return pl.ds(pl.multiple_of(start, size), size)

    def block_rows(i):
        return span(i * BLOCK, BLOCK)

    def load(i, role):
        block = odd if role == 0 else 1 - odd
        src, dst = ((k_hbm, k_ref), (v_hbm, v_ref), (mod_hbm, mod_ref), (q_hbm, q_ref))[i]
        if i == 2:
            src, dst = src.at[block], dst.at[role]
        else:
            src, dst = src.at[block_rows(block)], dst.at[pl.ds(role * BLOCK, BLOCK)]
        return pltpu.make_async_copy(src, dst, load_sem.at[i, role])

    def loaded(i):
        load(i, 0).wait()
        load(i, 1).wait()

    for i in range(4):
        load(i, 0).start()
        load(i, 1).start()

    def half_rows(upper):
        return span(upper * half, half)

    def quarter_rows(upper, lower):
        return span(upper * half + lower * quarter, quarter)

    def own_half(b, part):
        node[b, part, half_rows(bit(b - 1)), :] = pair_means(node[b - 1, part])

    def other_half(b, part):
        node[b, part, half_rows(1 - bit(b - 1)), :] = pair_means(far[b - 1, part])

    loaded(0)
    loaded(1)
    ones = [pair_means(own[part][...]) for part in range(2)]
    twos = [pair_means(one) for one in ones]
    threes = [pair_means(two) for two in twos]
    for part in range(2):
        node[1, part, half_rows(odd), :] = twos[part]
        node[2, part, quarter_rows(bit(1), odd), :] = threes[part]

    @pl.when(~takes)
    def _():
        cross[...] = jnp.zeros(cross.shape, BF16)
        cross_mod[...] = jnp.full(cross_mod.shape, -1, jnp.int32)

    pl.semaphore_wait(barrier, jnp.where(middle, levels, levels - 1))

    @pl.when(middle)
    def _():
        for target in (flip(1), across):
            pl.semaphore_signal(ready.at[levels], inc=1, device_id=place(target), device_id_type=MESH)

    def greet(b):
        if b > 0:
            pl.semaphore_wait(ready.at[b - 1], 1)
        if b < levels:
            pl.semaphore_signal(ready.at[b], inc=1, device_id=place(flip(b)), device_id_type=MESH)

    def remote(src, dst, send, recv, target):
        return pltpu.make_async_remote_copy(
            src_ref=src, dst_ref=dst, send_sem=send, recv_sem=recv,
            device_id=place(target), device_id_type=MESH,
        )

    def level_copy(b, part, slot, view, target, src=None):
        src = node if src is None else src
        return remote(src.at[b, part, view], far.at[b, part, view],
                      far_send.at[b, part, slot], far_recv.at[b, part, slot], target)

    def whole_copy(b, part):
        return level_copy(b, part, 0, pl.ds(0, BLOCK), flip(b))

    def half_copy(b, part, slot):
        start, size = (0, half // 4) if slot == 0 else (half // 4, half - half // 4)
        view = pl.ds(pl.multiple_of(bit(b - 1) * half + start, half // 4), size)
        return level_copy(b, part, 2 * slot, view, flip(b))

    def share_copy(b, part):
        return level_copy(b, part, 1, half_rows(bit(b - 1)), flip(b - 1), far)

    def five_view(slot):
        return quarter_rows(bit(3), bit(2) if slot == 0 else 1 - bit(2))

    def piece_view(b, slot):
        return quarter_rows(bit(1), odd if slot == 0 else 1 - odd) if b == 2 else five_view(slot)

    def piece_copy(b, part, slot):
        return level_copy(b, part, slot, piece_view(b, slot), flip(b))

    def piece_share(b, part, slot):
        return level_copy(b, part, 2 + slot, piece_view(b, slot), flip(b - 1), far)

    def three_copy(part):
        view = node.at[2, part, piece_view(2, 0)]
        return remote(view, view, mate_send.at[part, 2], mate_recv.at[part, 2], flip(0))

    def mate_copy(part, role):
        view = pl.ds(role * BLOCK, BLOCK)
        return remote(own[part].at[view], mate.at[part, view],
                      mate_send.at[part, role], mate_recv.at[part, role], flip(0))

    def last_copy(i):
        view = pl.ds(BLOCK + i * half, half)
        return remote(v_ref.at[view], mate.at[1, view],
                      mate_send.at[1 + i, 1], mate_recv.at[1 + i, 1], flip(0))

    def mod_copy():
        return remote(mod_ref, mate_mod, mate_send.at[2, 0], mate_recv.at[2, 0], flip(0))

    def hop_copy(part):
        return remote(mate.at[part, pl.ds(0, BLOCK)], cross.at[part],
                      cross_send.at[part], cross_recv.at[part], hop_out)

    def hop_mod():
        return remote(mate_mod.at[0], cross_mod, cross_send.at[2], cross_recv.at[2], hop_out)

    loaded(2)
    for part in range(2):
        three_copy(part).start()
    both(lambda part: half_copy(1, part, 0).start())
    mod_copy().start()
    for part in range(2):
        mate_copy(part, 0).start()
    greet(0)
    pl.semaphore_wait(ready.at[levels], 1)
    for part in range(2):
        piece_copy(2, part, 0).start()
    both(lambda part: half_copy(1, part, 1).start())
    loaded(3)

    def label_rows(i):
        return jnp.broadcast_to(mod_ref[i].astype(F32), (BLOCK, BLOCK))

    labels = [label_rows(0), label_rows(1)]
    columns = [jnp.transpose(x) for x in labels]
    zero = jnp.zeros((BLOCK, BLOCK), F32)
    for i in range(2):
        for j in range(2):
            value = zero if i == j else jnp.where(labels[j] == columns[i], 0.0, -jnp.inf)
            bias_own[i * BLOCK : (i + 1) * BLOCK, j * BLOCK : (j + 1) * BLOCK] = value

    def head_cols(h):
        return pl.ds(pl.multiple_of(h * HEAD_DIM, HEAD_DIM), HEAD_DIM)

    def score(q, k):
        return lax.dot_general(q, k, (((1,), (1,)), ((), ())), preferred_element_type=F32) * scale

    def first(h):
        cols = head_cols(h)
        s = score(q_ref[:, cols], k_ref[:, cols]) + bias_own[...]
        m = jnp.broadcast_to(jnp.max(s, axis=1, keepdims=True), (rows, BLOCK))
        p0 = jnp.exp2(s[:, :BLOCK] - m)
        p1 = jnp.exp2(s[:, BLOCK:] - m)
        m_ref[h] = m
        l_ref[h] = p0 + p1
        p = jnp.concatenate([p0.astype(BF16), p1.astype(BF16)], axis=1)
        acc_ref[h] = jnp.dot(p, v_ref[:, cols], preferred_element_type=F32)

    def merged(h, view, sources):
        cols = head_cols(h)
        q = q_ref[view, cols]
        scores = []
        for k, v in sources:
            scores.append(score(q, k[:, cols]))
        best = functools.reduce(jnp.maximum, scores)
        m_old = m_ref[h, view]
        m = jnp.maximum(m_old, jnp.max(best, axis=1, keepdims=True))
        a = jnp.exp2(m_old - m)
        weights = [jnp.exp2(s - m) for s in scores]
        l = l_ref[h, view] * a + functools.reduce(jnp.add, weights)
        p = jnp.concatenate([w.astype(BF16) for w in weights], axis=1)
        rows_in = jnp.concatenate([v[:, cols] for k, v in sources], axis=0)
        acc = acc_ref[h, view] * a + jnp.dot(p, rows_in, preferred_element_type=F32)
        return m, l, acc

    def update(h, view, sources):
        m, l, acc = merged(h, view, sources)
        m_ref[h, view] = m
        l_ref[h, view] = l
        acc_ref[h, view] = acc

    def weigh(h):
        cols = head_cols(h)
        q = q_ref[:, cols]
        s = score(q, jnp.concatenate([cross[0, :, cols], mate[0, BLOCK:rows, cols]], axis=0))
        near = jnp.concatenate([s[:BLOCK, :BLOCK], s[BLOCK:, BLOCK:]], axis=0) + bias_near[...]
        coarse = score(q, far[0, 0, :, cols])
        m_old = m_ref[h]
        m = jnp.maximum(m_old, jnp.max(jnp.maximum(near, coarse), axis=1, keepdims=True))
        a = jnp.exp2(m_old - m)
        near = jnp.exp2(near - m)
        coarse = jnp.exp2(coarse - m)
        total = jnp.sum(l_ref[h] * a + near + coarse, axis=1, keepdims=True)
        l_ref[h] = jnp.broadcast_to(1.0 / total, (rows, HEAD_DIM))
        acc_ref[h] = acc_ref[h] * a
        near = near.astype(BF16)
        none = jnp.zeros((BLOCK, BLOCK), BF16)
        p_near[h, 0:BLOCK, :] = jnp.concatenate([near[:BLOCK], none], axis=1)
        p_near[h, BLOCK:rows, :] = jnp.concatenate([none, near[BLOCK:]], axis=1)
        p_coarse[h] = coarse.astype(BF16)

    def finish(h):
        cols = head_cols(h)
        beside = jnp.concatenate([cross[1, :, cols], mate[1, BLOCK:rows, cols]], axis=0)
        acc = acc_ref[h] + jnp.dot(p_near[h], beside, preferred_element_type=F32)
        acc = acc + jnp.dot(p_coarse[h], far[0, 1, :, cols], preferred_element_type=F32)
        acc = acc * l_ref[h]
        one, two = acc[:BLOCK], acc[BLOCK:]
        out_ref[0:BLOCK, cols] = jnp.where(odd == 0, one, two).astype(BF16)
        out_ref[BLOCK:rows, cols] = jnp.where(odd == 0, two, one).astype(BF16)

    def every_head(body, low=0, high=heads):
        def step(h, carry):
            body(h)
            return carry

        lax.fori_loop(low, high, step, 0, unroll=8)

    everything = pl.ds(0, rows)

    def near_bias(role, label):
        other = jnp.broadcast_to(label.astype(F32), (BLOCK, BLOCK))
        mine = jnp.transpose(label_rows(role))
        bias_near[role * BLOCK : (role + 1) * BLOCK, :] = jnp.where(other == mine, 0.0, -jnp.inf)

    def level_rows(b):
        return (far.at[b, 0], far.at[b, 1])

    def coarse_mate(part, role):
        far[0, part, role * half : (role + 1) * half, :] = pair_means(
            mate[part, role * BLOCK : (role + 1) * BLOCK, :]
        )

    def pair_three(part):
        three_copy(part).wait_recv()
        piece_copy(2, part, 1).start()

    def share_two(part):
        half_copy(1, part, 0).wait_recv()
        half_copy(1, part, 1).wait_recv()
        share_copy(1, part).start()

    def share_three(part, slot):
        piece_copy(2, part, slot).wait_recv()
        piece_share(2, part, slot).start()

    def send_five(part, slot):
        if levels > 4:
            half_of = half_rows(bit(2) if slot == 0 else 1 - bit(2))
            node[4, part, five_view(slot), :] = pair_means(node[3, part, half_of, :])
            piece_copy(4, part, slot).start()

    def two_ready(part):
        share_copy(1, part).wait_recv()
        other_half(2, part)
        own_half(3, part)
        send_five(part, 0)

    def three_ready(part):
        for slot in range(2):
            piece_share(2, part, slot).wait_recv()
        other_half(3, part)
        whole_copy(3, part).start()
        send_five(part, 1)

    def four_ready(part):
        whole_copy(3, part).wait_recv()
        if levels > 5:
            other_half(4, part)
            own_half(5, part)

    def share_five(slot):
        if levels > 4:
            for part in range(2):
                piece_copy(4, part, slot).wait_recv()
                piece_share(4, part, slot).start()

    def relay(part):
        mate_copy(part, 0).wait_recv()

        @pl.when(gives)
        def _():
            if part == 0:
                hop_mod().start()
            hop_copy(part).start()

    parts = 2

    def first_part(i):
        every_head(first, heads * i // parts, heads * (i + 1) // parts)

    first_part(0)
    greet(1)
    both(pair_three)
    greet(2)
    first_part(1)
    both(lambda part: share_three(part, 0))
    greet(3)
    both(share_two)
    mate_copy(0, 1).start()
    both(lambda i: last_copy(i).start())
    for b in range(4, levels + 1):
        greet(b)
    mod_copy().wait_recv()
    relay(0)
    coarse_mate(0, 0)
    both(lambda part: share_three(part, 1))
    relay(1)
    coarse_mate(1, 0)
    near_bias(1, mate_mod[1])
    both(two_ready)
    every_head(lambda h: update(h, everything, [level_rows(1)]))
    both(three_ready)
    share_five(0)
    every_head(lambda h: update(h, everything, [level_rows(2)]))
    both(four_ready)
    every_head(lambda h: update(h, everything, [level_rows(3)]))
    mate_copy(0, 1).wait_recv()
    coarse_mate(0, 1)
    share_five(1)

    @pl.when(takes)
    def _():
        hop_mod().wait_recv()
        hop_copy(0).wait_recv()

    near_bias(0, cross_mod[...])
    last = []
    if levels > 4:
        for slot in range(2):
            both(lambda part: piece_share(4, part, slot).wait_recv())
        last.append(level_rows(4))
    for b in range(5, levels):
        for part in range(2):
            other_half(b, part)
            whole_copy(b, part).start()
            whole_copy(b, part).wait_recv()
            if b + 1 < levels:
                own_half(b + 1, part)
        last.append(level_rows(b))
    if last:
        every_head(lambda h: update(h, everything, last))
    every_head(weigh)
    pl.when(takes)(lambda: hop_copy(1).wait_recv())
    for i in range(2):
        last_copy(i).wait_recv()
        far[0, 1, half + i * quarter : half + (i + 1) * quarter, :] = pair_means(
            mate[1, BLOCK + i * half : BLOCK + (i + 1) * half, :]
        )
    every_head(finish)

    @pl.when(gives)
    def _():
        both(lambda part: hop_copy(part).wait_send())
        hop_mod().wait_send()

    mod_copy().wait_send()
    mate_copy(0, 1).wait_send()
    for part in range(2):
        three_copy(part).wait_send()
        mate_copy(part, 0).wait_send()
        last_copy(part).wait_send()
        half_copy(1, part, 0).wait_send()
        half_copy(1, part, 1).wait_send()
        share_copy(1, part).wait_send()
        whole_copy(3, part).wait_send()
        for b in (2, 4):
            for slot in range(2):
                if b < levels:
                    piece_copy(b, part, slot).wait_send()
                    piece_share(b, part, slot).wait_send()
        for b in range(5, levels):
            whole_copy(b, part).wait_send()


def shards(levels, inner, queries, keys, values, modality):
    rows, width = queries.shape
    heads = width // HEAD_DIM
    labels = modality.reshape(rows // BLOCK, 1, BLOCK)
    hbm = pl.BlockSpec(memory_space=pl.ANY)
    state = pltpu.VMEM((heads, rows, HEAD_DIM), F32)
    shard = pltpu.VMEM((rows, width), BF16)
    level = pltpu.VMEM((levels, 2, BLOCK, width), BF16)
    label = pltpu.VMEM((rows // BLOCK, 1, BLOCK), jnp.int32)
    return pl.pallas_call(
        functools.partial(kernel, levels, inner),
        out_shape=pltpu.VMEM((rows, width), BF16),
        in_specs=[hbm] * 4,
        out_specs=pl.BlockSpec(memory_space=pltpu.VMEM),
        scratch_shapes=[
            shard,
            shard,
            shard,
            label,
            level,
            level,
            pltpu.VMEM((2, rows, width), BF16),
            label,
            pltpu.VMEM((2, BLOCK, width), BF16),
            pltpu.VMEM((1, BLOCK), jnp.int32),
            pltpu.VMEM((rows, 2 * BLOCK), F32),
            pltpu.VMEM((rows, BLOCK), F32),
            state,
            state,
            state,
            pltpu.VMEM((heads, rows, 2 * BLOCK), BF16),
            pltpu.VMEM((heads, rows, BLOCK), BF16),
            pltpu.SemaphoreType.REGULAR((levels + 1,)),
            pltpu.SemaphoreType.DMA((4, 2)),
            pltpu.SemaphoreType.DMA((levels, 2, 4)),
            pltpu.SemaphoreType.DMA((levels, 2, 4)),
            pltpu.SemaphoreType.DMA((3, 3)),
            pltpu.SemaphoreType.DMA((3, 3)),
            pltpu.SemaphoreType.DMA((3,)),
            pltpu.SemaphoreType.DMA((3,)),
        ],
        compiler_params=pltpu.CompilerParams(
            collective_id=0, has_side_effects=True, vmem_limit_bytes=56 * 2**20
        ),
    )(queries, keys, values, labels)


def solution(mesh):
    outer, inner = mesh.shape["outer"], mesh.shape["inner"]
    levels = (outer * inner).bit_length() - 1
    rows = P(AXES, None)
    return jax.shard_map(
        functools.partial(shards, levels, inner),
        mesh=mesh,
        in_specs=(rows, rows, rows, P(AXES)),
        out_specs=rows,
        check_vma=False,
    )
```

```python
import functools
import math

import jax
import jax.numpy as jnp
from jax import lax
from jax.experimental import pallas as pl
from jax.experimental.pallas import tpu as pltpu
from jax.sharding import PartitionSpec as P

HEAD_DIM = 128
BLOCK = 128
AXES = ("outer", "inner")
MESH = pl.DeviceIdType.MESH
F32 = jnp.float32
BF16 = jnp.bfloat16


def pair_means(rows):
    half = rows.shape[0] // 2
    r = lax.broadcasted_iota(jnp.int32, (half, rows.shape[0]), 0)
    c = lax.broadcasted_iota(jnp.int32, (half, rows.shape[0]), 1)
    mix = jnp.where(c // 2 == r, 0.5, 0.0).astype(BF16)
    return jnp.dot(mix, rows, preferred_element_type=F32).astype(BF16)


def kernel(
    levels, inner, q_hbm, k_hbm, v_hbm, mod_hbm, out_ref,
    q_ref, k_ref, v_ref, mod_ref, node, far, mate, mate_mod, cross, cross_mod,
    bias_own, bias_near, m_ref, l_ref, acc_ref, p_near, p_coarse,
    ready, load_sem, far_send, far_recv, mate_send, mate_recv, cross_send, cross_recv,
):
    rows, width = q_ref.shape
    heads = width // HEAD_DIM
    half = BLOCK // 2
    quarter = BLOCK // 4
    count = 2**levels
    me = lax.axis_index("outer") * inner + lax.axis_index("inner")
    scale = HEAD_DIM**-0.5 * math.log2(math.e)
    own = (k_ref, v_ref)

    def place(d):
        return (d // inner, d % inner)

    def bit(b):
        return me // 2**b % 2

    def flip(b):
        return me + 2**b * (1 - 2 * bit(b))

    odd = bit(0)
    hop_out = jnp.where(odd == 0, (me + 2) % count, (me + count - 2) % count)
    gives = ((odd == 0) & (me + 2 < count)) | ((odd == 1) & (me > 2))
    takes = ((odd == 0) & (me > 0)) | ((odd == 1) & (me + 1 < count))

    barrier = pltpu.get_barrier_semaphore()
    for b in range(levels):
        if b != 2:
            pl.semaphore_signal(barrier, inc=1, device_id=place(flip(b)), device_id_type=MESH)
    middle = bit(1) != bit(2)
    across = me + 2 * (1 - 2 * bit(1)) + 4 * (1 - 2 * bit(2))

    @pl.when(middle)
    def _():
        pl.semaphore_signal(barrier, inc=1, device_id=place(across), device_id_type=MESH)


    def both(action):
        for part in range(2):
            action(part)

    def span(start, size):
        return pl.ds(pl.multiple_of(start, size), size)

    def block_rows(i):
        return span(i * BLOCK, BLOCK)

    def load(i, role):
        block = odd if role == 0 else 1 - odd
        src, dst = ((k_hbm, k_ref), (v_hbm, v_ref), (mod_hbm, mod_ref), (q_hbm, q_ref))[i]
        if i == 2:
            src, dst = src.at[block], dst.at[role]
        else:
            src, dst = src.at[block_rows(block)], dst.at[pl.ds(role * BLOCK, BLOCK)]
        return pltpu.make_async_copy(src, dst, load_sem.at[i, role])

    def loaded(i):
        load(i, 0).wait()
        load(i, 1).wait()

    for i in range(4):
        load(i, 0).start()
        load(i, 1).start()

    def half_rows(upper):
        return span(upper * half, half)

    def quarter_rows(upper, lower):
        return span(upper * half + lower * quarter, quarter)

    def own_half(b, part):
        node[b, part, half_rows(bit(b - 1)), :] = pair_means(node[b - 1, part])

    def other_half(b, part):
        node[b, part, half_rows(1 - bit(b - 1)), :] = pair_means(far[b - 1, part])

    loaded(0)
    loaded(1)
    ones = [pair_means(own[part][...]) for part in range(2)]
    twos = [pair_means(one) for one in ones]
    threes = [pair_means(two) for two in twos]
    for part in range(2):
        node[1, part, half_rows(odd), :] = twos[part]
        node[2, part, quarter_rows(bit(1), odd), :] = threes[part]

    @pl.when(~takes)
    def _():
        cross[...] = jnp.zeros(cross.shape, BF16)
        cross_mod[...] = jnp.full(cross_mod.shape, -1, jnp.int32)

    pl.semaphore_wait(barrier, jnp.where(middle, levels, levels - 1))

    @pl.when(middle)
    def _():
        for target in (flip(1), across):
            pl.semaphore_signal(ready.at[levels], inc=1, device_id=place(target), device_id_type=MESH)

    def greet(b):
        if b > 0:
            pl.semaphore_wait(ready.at[b - 1], 1)
        if b < levels:
            pl.semaphore_signal(ready.at[b], inc=1, device_id=place(flip(b)), device_id_type=MESH)

    def remote(src, dst, send, recv, target):
        return pltpu.make_async_remote_copy(
            src_ref=src, dst_ref=dst, send_sem=send, recv_sem=recv,
            device_id=place(target), device_id_type=MESH,
        )

    def level_copy(b, part, slot, view, target, src=None):
        src = node if src is None else src
        return remote(src.at[b, part, view], far.at[b, part, view],
                      far_send.at[b, part, slot], far_recv.at[b, part, slot], target)

    def whole_copy(b, part):
        return level_copy(b, part, 0, pl.ds(0, BLOCK), flip(b))

    def half_copy(b, part, slot):
        start, size = (0, half // 4) if slot == 0 else (half // 4, half - half // 4)
        view = pl.ds(pl.multiple_of(bit(b - 1) * half + start, half // 4), size)
        return level_copy(b, part, 2 * slot, view, flip(b))

    def share_copy(b, part):
        return level_copy(b, part, 1, half_rows(bit(b - 1)), flip(b - 1), far)

    def five_view(slot):
        return quarter_rows(bit(3), bit(2) if slot == 0 else 1 - bit(2))

    def piece_view(b, slot):
        return quarter_rows(bit(1), odd if slot == 0 else 1 - odd) if b == 2 else five_view(slot)

    def piece_copy(b, part, slot):
        return level_copy(b, part, slot, piece_view(b, slot), flip(b))

    def piece_share(b, part, slot):
        return level_copy(b, part, 2 + slot, piece_view(b, slot), flip(b - 1), far)

    def three_copy(part):
        view = node.at[2, part, piece_view(2, 0)]
        return remote(view, view, mate_send.at[part, 2], mate_recv.at[part, 2], flip(0))

    def mate_copy(part, role):
        view = pl.ds(role * BLOCK, BLOCK)
        return remote(own[part].at[view], mate.at[part, view],
                      mate_send.at[part, role], mate_recv.at[part, role], flip(0))

    def last_copy(part, i):
        slot = (part, 1) if i == 0 else (2, 2 - part)
        view = pl.ds(BLOCK + i * half, half)
        return remote(own[part].at[view], mate.at[part, view],
                      mate_send.at[slot], mate_recv.at[slot], flip(0))

    def mod_copy():
        return remote(mod_ref, mate_mod, mate_send.at[2, 0], mate_recv.at[2, 0], flip(0))

    def hop_copy(part):
        return remote(mate.at[part, pl.ds(0, BLOCK)], cross.at[part],
                      cross_send.at[part], cross_recv.at[part], hop_out)

    def hop_mod():
        return remote(mate_mod.at[0], cross_mod, cross_send.at[2], cross_recv.at[2], hop_out)

    loaded(2)
    for part in range(2):
        three_copy(part).start()
    both(lambda part: half_copy(1, part, 0).start())
    mod_copy().start()
    for part in range(2):
        mate_copy(part, 0).start()
    greet(0)
    pl.semaphore_wait(ready.at[levels], 1)
    for part in range(2):
        piece_copy(2, part, 0).start()
    both(lambda part: half_copy(1, part, 1).start())
    loaded(3)

    def label_rows(i):
        return jnp.broadcast_to(mod_ref[i].astype(F32), (BLOCK, BLOCK))

    labels = [label_rows(0), label_rows(1)]
    columns = [jnp.transpose(x) for x in labels]
    zero = jnp.zeros((BLOCK, BLOCK), F32)
    for i in range(2):
        for j in range(2):
            value = zero if i == j else jnp.where(labels[j] == columns[i], 0.0, -jnp.inf)
            bias_own[i * BLOCK : (i + 1) * BLOCK, j * BLOCK : (j + 1) * BLOCK] = value

    def head_cols(h):
        return pl.ds(pl.multiple_of(h * HEAD_DIM, HEAD_DIM), HEAD_DIM)

    def score(q, k):
        return lax.dot_general(q, k, (((1,), (1,)), ((), ())), preferred_element_type=F32) * scale

    def first(h):
        cols = head_cols(h)
        s = score(q_ref[:, cols], k_ref[:, cols]) + bias_own[...]
        m = jnp.broadcast_to(jnp.max(s, axis=1, keepdims=True), (rows, BLOCK))
        p0 = jnp.exp2(s[:, :BLOCK] - m)
        p1 = jnp.exp2(s[:, BLOCK:] - m)
        m_ref[h] = m
        l_ref[h] = p0 + p1
        p = jnp.concatenate([p0.astype(BF16), p1.astype(BF16)], axis=1)
        acc_ref[h] = jnp.dot(p, v_ref[:, cols], preferred_element_type=F32)

    def merged(h, view, sources):
        cols = head_cols(h)
        q = q_ref[view, cols]
        scores = []
        for k, v in sources:
            scores.append(score(q, k[:, cols]))
        best = functools.reduce(jnp.maximum, scores)
        m_old = m_ref[h, view]
        m = jnp.maximum(m_old, jnp.max(best, axis=1, keepdims=True))
        a = jnp.exp2(m_old - m)
        weights = [jnp.exp2(s - m) for s in scores]
        l = l_ref[h, view] * a + functools.reduce(jnp.add, weights)
        p = jnp.concatenate([w.astype(BF16) for w in weights], axis=1)
        rows_in = jnp.concatenate([v[:, cols] for k, v in sources], axis=0)
        acc = acc_ref[h, view] * a + jnp.dot(p, rows_in, preferred_element_type=F32)
        return m, l, acc

    def update(h, view, sources):
        m, l, acc = merged(h, view, sources)
        m_ref[h, view] = m
        l_ref[h, view] = l
        acc_ref[h, view] = acc

    def weigh(h):
        cols = head_cols(h)
        q = q_ref[:, cols]
        s = score(q, jnp.concatenate([cross[0, :, cols], mate[0, BLOCK:rows, cols]], axis=0))
        near = jnp.concatenate([s[:BLOCK, :BLOCK], s[BLOCK:, BLOCK:]], axis=0) + bias_near[...]
        coarse = score(q, far[0, 0, :, cols])
        m_old = m_ref[h]
        m = jnp.maximum(m_old, jnp.max(jnp.maximum(near, coarse), axis=1, keepdims=True))
        a = jnp.exp2(m_old - m)
        near = jnp.exp2(near - m)
        coarse = jnp.exp2(coarse - m)
        total = jnp.sum(l_ref[h] * a + near + coarse, axis=1, keepdims=True)
        l_ref[h] = jnp.broadcast_to(1.0 / total, (rows, HEAD_DIM))
        acc_ref[h] = acc_ref[h] * a
        near = near.astype(BF16)
        none = jnp.zeros((BLOCK, BLOCK), BF16)
        p_near[h, 0:BLOCK, :] = jnp.concatenate([near[:BLOCK], none], axis=1)
        p_near[h, BLOCK:rows, :] = jnp.concatenate([none, near[BLOCK:]], axis=1)
        p_coarse[h] = coarse.astype(BF16)

    def finish(h):
        cols = head_cols(h)
        beside = jnp.concatenate([cross[1, :, cols], mate[1, BLOCK:rows, cols]], axis=0)
        acc = acc_ref[h] + jnp.dot(p_near[h], beside, preferred_element_type=F32)
        acc = acc + jnp.dot(p_coarse[h], far[0, 1, :, cols], preferred_element_type=F32)
        acc = acc * l_ref[h]
        one, two = acc[:BLOCK], acc[BLOCK:]
        out_ref[0:BLOCK, cols] = jnp.where(odd == 0, one, two).astype(BF16)
        out_ref[BLOCK:rows, cols] = jnp.where(odd == 0, two, one).astype(BF16)

    def every_head(body, low=0, high=heads):
        def step(h, carry):
            body(h)
            return carry

        lax.fori_loop(low, high, step, 0, unroll=8)

    everything = pl.ds(0, rows)

    def near_bias(role, label):
        other = jnp.broadcast_to(label.astype(F32), (BLOCK, BLOCK))
        mine = jnp.transpose(label_rows(role))
        bias_near[role * BLOCK : (role + 1) * BLOCK, :] = jnp.where(other == mine, 0.0, -jnp.inf)

    def level_rows(b):
        return (far.at[b, 0], far.at[b, 1])

    def coarse_mate(part, role):
        far[0, part, role * half : (role + 1) * half, :] = pair_means(
            mate[part, role * BLOCK : (role + 1) * BLOCK, :]
        )

    def last_mate(part):
        for i in range(2):
            last_copy(part, i).wait_recv()
            far[0, part, half + i * quarter : half + (i + 1) * quarter, :] = pair_means(
                mate[part, BLOCK + i * half : BLOCK + (i + 1) * half, :]
            )

    def pair_three(part):
        three_copy(part).wait_recv()
        piece_copy(2, part, 1).start()

    def share_two(part):
        half_copy(1, part, 0).wait_recv()
        half_copy(1, part, 1).wait_recv()
        share_copy(1, part).start()

    def share_three(part, slot):
        piece_copy(2, part, slot).wait_recv()
        piece_share(2, part, slot).start()

    def send_five(part, slot):
        if levels > 4:
            half_of = half_rows(bit(2) if slot == 0 else 1 - bit(2))
            node[4, part, five_view(slot), :] = pair_means(node[3, part, half_of, :])
            piece_copy(4, part, slot).start()

    def two_ready(part):
        share_copy(1, part).wait_recv()
        other_half(2, part)
        own_half(3, part)
        send_five(part, 0)

    def three_ready(part):
        for slot in range(2):
            piece_share(2, part, slot).wait_recv()
        other_half(3, part)
        whole_copy(3, part).start()
        send_five(part, 1)

    def four_ready(part):
        whole_copy(3, part).wait_recv()
        if levels > 5:
            other_half(4, part)
            own_half(5, part)

    def share_five(slot):
        if levels > 4:
            for part in range(2):
                piece_copy(4, part, slot).wait_recv()
                piece_share(4, part, slot).start()

    def relay(part):
        mate_copy(part, 0).wait_recv()

        @pl.when(gives)
        def _():
            if part == 0:
                hop_mod().start()
            hop_copy(part).start()

    parts = 2

    def first_part(i):
        every_head(first, heads * i // parts, heads * (i + 1) // parts)

    first_part(0)
    greet(1)
    both(pair_three)
    greet(2)
    first_part(1)
    both(lambda part: share_three(part, 0))
    greet(3)
    both(share_two)
    for part in range(2):
        both(lambda i: last_copy(part, i).start())
    for b in range(4, levels + 1):
        greet(b)
    mod_copy().wait_recv()
    relay(0)
    coarse_mate(0, 0)
    both(lambda part: share_three(part, 1))
    relay(1)
    coarse_mate(1, 0)
    near_bias(1, mate_mod[1])
    both(two_ready)
    every_head(lambda h: update(h, everything, [level_rows(1)]))
    both(three_ready)
    share_five(0)
    every_head(lambda h: update(h, everything, [level_rows(2)]))
    both(four_ready)
    every_head(lambda h: update(h, everything, [level_rows(3)]))
    last_mate(0)
    share_five(1)

    @pl.when(takes)
    def _():
        hop_mod().wait_recv()
        hop_copy(0).wait_recv()

    near_bias(0, cross_mod[...])
    last = []
    if levels > 4:
        for slot in range(2):
            both(lambda part: piece_share(4, part, slot).wait_recv())
        last.append(level_rows(4))
    for b in range(5, levels):
        for part in range(2):
            other_half(b, part)
            whole_copy(b, part).start()
            whole_copy(b, part).wait_recv()
            if b + 1 < levels:
                own_half(b + 1, part)
        last.append(level_rows(b))
    if last:
        every_head(lambda h: update(h, everything, last))
    every_head(weigh)
    pl.when(takes)(lambda: hop_copy(1).wait_recv())
    last_mate(1)
    every_head(finish)

    @pl.when(gives)
    def _():
        both(lambda part: hop_copy(part).wait_send())
        hop_mod().wait_send()

    mod_copy().wait_send()
    for part in range(2):
        three_copy(part).wait_send()
        mate_copy(part, 0).wait_send()
        both(lambda i: last_copy(part, i).wait_send())
        half_copy(1, part, 0).wait_send()
        half_copy(1, part, 1).wait_send()
        share_copy(1, part).wait_send()
        whole_copy(3, part).wait_send()
        for b in (2, 4):
            for slot in range(2):
                if b < levels:
                    piece_copy(b, part, slot).wait_send()
                    piece_share(b, part, slot).wait_send()
        for b in range(5, levels):
            whole_copy(b, part).wait_send()


def shards(levels, inner, queries, keys, values, modality):
    rows, width = queries.shape
    heads = width // HEAD_DIM
    labels = modality.reshape(rows // BLOCK, 1, BLOCK)
    hbm = pl.BlockSpec(memory_space=pl.ANY)
    state = pltpu.VMEM((heads, rows, HEAD_DIM), F32)
    shard = pltpu.VMEM((rows, width), BF16)
    level = pltpu.VMEM((levels, 2, BLOCK, width), BF16)
    label = pltpu.VMEM((rows // BLOCK, 1, BLOCK), jnp.int32)
    return pl.pallas_call(
        functools.partial(kernel, levels, inner),
        out_shape=pltpu.VMEM((rows, width), BF16),
        in_specs=[hbm] * 4,
        out_specs=pl.BlockSpec(memory_space=pltpu.VMEM),
        scratch_shapes=[
            shard,
            shard,
            shard,
            label,
            level,
            level,
            pltpu.VMEM((2, rows, width), BF16),
            label,
            pltpu.VMEM((2, BLOCK, width), BF16),
            pltpu.VMEM((1, BLOCK), jnp.int32),
            pltpu.VMEM((rows, 2 * BLOCK), F32),
            pltpu.VMEM((rows, BLOCK), F32),
            state,
            state,
            state,
            pltpu.VMEM((heads, rows, 2 * BLOCK), BF16),
            pltpu.VMEM((heads, rows, BLOCK), BF16),
            pltpu.SemaphoreType.REGULAR((levels + 1,)),
            pltpu.SemaphoreType.DMA((4, 2)),
            pltpu.SemaphoreType.DMA((levels, 2, 4)),
            pltpu.SemaphoreType.DMA((levels, 2, 4)),
            pltpu.SemaphoreType.DMA((3, 3)),
            pltpu.SemaphoreType.DMA((3, 3)),
            pltpu.SemaphoreType.DMA((3,)),
            pltpu.SemaphoreType.DMA((3,)),
        ],
        compiler_params=pltpu.CompilerParams(
            collective_id=0, has_side_effects=True, vmem_limit_bytes=56 * 2**20
        ),
    )(queries, keys, values, labels)


def solution(mesh):
    outer, inner = mesh.shape["outer"], mesh.shape["inner"]
    levels = (outer * inner).bit_length() - 1
    rows = P(AXES, None)
    return jax.shard_map(
        functools.partial(shards, levels, inner),
        mesh=mesh,
        in_specs=(rows, rows, rows, P(AXES)),
        out_specs=rows,
        check_vma=False,
    )
```
